32 devices in a mesh: chan: 16 (over z, x, core), win: 2 (over y).
Axes of the slice: x: 2, y: 2, z: 4, core: 2. Of those that a mesh axis runs over, the one named last changes fastest.
Arguments:
- spectra: bfloat16 [8, 1024, 2, 2048], P('win', 'chan'), may hold values from -4.5 to 4.5
- owners: int32 [4], replicated, may hold values from 0 to 15
- blocks: int32 [4], replicated, may hold values from 0 to 3
- max_lag: int32 [4, 16, 1024], P(None, 'win', 'chan'), may hold values from 1 to 64
Outputs:
- correlations: float32 [4, 16, 1024, 128], P(None, 'win', 'chan')
The draws below stay inside these ranges and needn't reach their ends.
All inputs are finite; a program needn't handle non-finite values.
Results may differ from the reference program's by a relative error of at most 0.0034.
Values may be sent and summed in bfloat16 or wider, within the bound.
A program may use at most 128 MiB of HBM per device.

```python
import jax
import jax.numpy as jnp
from jax import lax

F = 2048
W_DEV = 4
SRC = 16
C_DEV = 64
STEPS = 4
LAGS = 128
CHANNELS = 1024
WINDOWS = 8
N_CHAN = 16
N_WIN = 2


def touch_ends(drawn, rng, smallest, top_value):
    longest = drawn.shape.index(max(drawn.shape))
    spots = []
    for shift in (0, 1):
        where = [jax.random.randint(jax.random.fold_in(rng, axis), (), 0, length) for axis, length in enumerate(drawn.shape)]
        where[longest] = (where[longest] + shift) % drawn.shape[longest]
        spots.append(tuple(where))
    return drawn.at[spots[0]].set(smallest).at[spots[1]].set(top_value)


def levels(stream_key, extent, pieces, low, top_value):
    gain = 1.0
    for dim, blocks in pieces:
        heights = jax.random.uniform(jax.random.fold_in(jax.random.fold_in(stream_key, 6), dim), (blocks,), jnp.float32, low / len(pieces), top_value / len(pieces))
        gain = gain * jnp.repeat(jnp.exp(heights), extent[dim] // blocks).reshape((-1,) + (1,) * (len(extent) - 1 - dim))
    return gain


def bell_draw(stream_key, shape, scale, limit, cuts=(), kind=jnp.bfloat16):
    array = jax.random.normal(stream_key, shape, jnp.float32) * scale
    if len(cuts) > 0:
        array = levels(stream_key, shape, cuts, -0.22, 0.18) * array
    return jnp.clip(array, min=-limit, max=limit).astype(kind)


def setup_inputs(seed: int = 0) -> dict:
    key_list = jax.random.split(jax.random.key(seed), 5)
    spectra = bell_draw(key_list[0], (WINDOWS, CHANNELS, 2, F), 0.7, 4.5, ((0, 2), (1, 16)))
    owners = touch_ends(jax.random.randint(key_list[1], (STEPS,), 0, N_CHAN), jax.random.fold_in(key_list[1], 1), 0, N_CHAN - 1).astype(jnp.int32)
    blocks = touch_ends(jax.random.randint(key_list[2], (STEPS,), 0, C_DEV // SRC), jax.random.fold_in(key_list[2], 1), 0, (C_DEV // SRC) - 1).astype(jnp.int32)
    max_lag = touch_ends(jax.random.randint(key_list[3], (STEPS, SRC, CHANNELS), 1, LAGS // 2 + 1), jax.random.fold_in(key_list[3], 1), 1, (LAGS // 2 + 1) - 1).astype(jnp.int32)
    return dict(spectra=spectra, owners=owners, blocks=blocks, max_lag=max_lag)


def lag_table(bin_count, lag_count, window_count):
    bins = jnp.arange(bin_count, dtype=jnp.int32)[:, None]
    offsets = jnp.arange(lag_count, dtype=jnp.int32)[None, :] - lag_count // 2
    phase = (bins * offsets % (2 * bin_count)).astype(jnp.float32) * (jnp.pi / bin_count)
    weight = jnp.where(bins == 0, 1.0, 2.0).astype(jnp.float32) / jnp.sqrt(jnp.float32(2.0 * bin_count * window_count))
    return jnp.concatenate([weight * jnp.cos(phase), -weight * jnp.sin(phase)], 0).astype(jnp.bfloat16)

def cross_spectra(source_block, receivers):
    a_real = source_block[:, :, 0].astype(jnp.float32)
    a_imag = source_block[:, :, 1].astype(jnp.float32)
    b_real = receivers[:, :, 0].astype(jnp.float32)
    b_imag = receivers[:, :, 1].astype(jnp.float32)
    real_part = jnp.einsum('wsf,wcf->scf', a_real, b_real) + jnp.einsum('wsf,wcf->scf', a_imag, b_imag)
    imag_part = jnp.einsum('wsf,wcf->scf', a_imag, b_real) - jnp.einsum('wsf,wcf->scf', a_real, b_imag)
    return jnp.stack([real_part, imag_part], 2).astype(jnp.bfloat16)

def reference(spectra, owners, blocks, max_lag):
    lag_matrix = lag_table(F, LAGS, W_DEV * N_WIN)
    grouped = spectra.reshape(N_WIN, W_DEV, N_CHAN, C_DEV, 2, F).transpose(2, 0, 1, 3, 4, 5)
    offsets = jnp.abs(jnp.arange(LAGS, dtype=jnp.int32) - LAGS // 2)
    results = []
    for step_index in range(STEPS):
        first_channel = (owners[step_index] * C_DEV + blocks[step_index] * SRC).astype(jnp.int32)
        source_all = lax.dynamic_slice_in_dim(spectra, first_channel, SRC, 1)
        source_groups = source_all.reshape(N_WIN, W_DEV, SRC, 2, F)

        def one_block(receivers):
            summed_parts = jnp.zeros((SRC, C_DEV, LAGS), jnp.float32)
            for group in range(N_WIN):
                cross_part = cross_spectra(source_groups[group], receivers[group])
                flat = cross_part.reshape(SRC * C_DEV, 2 * F)
                summed_parts = summed_parts + jnp.dot(flat, lag_matrix, preferred_element_type=jnp.float32).reshape(SRC, C_DEV, LAGS)
            return summed_parts
        blocked = lax.map(one_block, grouped)
        whole = blocked.transpose(1, 0, 2, 3).reshape(SRC, CHANNELS, LAGS)
        inside = offsets[None, None, :] <= max_lag[step_index][:, :, None]
        results.append(jnp.where(inside, whole, jnp.float32(0.0)))
    return jnp.stack(results)
```

```python
import functools

import jax
import jax.numpy as jnp
import numpy as np
from jax import lax
from jax.experimental import pallas as pl
from jax.experimental.pallas import tpu as pltpu
from jax.sharding import PartitionSpec as P

SRC = 16
STEPS = 4
LAGS = 128
LANES = 128
PARTS = 4
PAIRED = 2


def lag_rows(bin_count, lag_count, window_count, slices):
    bins = np.arange(bin_count, dtype=np.int64)[None, :]
    offsets = np.arange(lag_count, dtype=np.int64)[:, None] - lag_count // 2
    phase = (bins * offsets % (2 * bin_count)) * (np.pi / bin_count)
    weight = np.where(bins == 0, 1.0, 2.0) / np.sqrt(2.0 * bin_count * window_count)
    rows = np.stack([weight * np.cos(phase), -weight * np.sin(phase)], 1)
    rows = rows.reshape(lag_count, 2, slices, bin_count // slices).transpose(2, 0, 1, 3)
    return rows.reshape(slices, lag_count, -1).astype(np.float32).astype(jnp.bfloat16)


def prepare_kernel(blocks_ref, spectra_ref, laid_ref, *, run):
    terms = 2 * spectra_ref.shape[0]
    bins = spectra_ref.shape[3]
    chunks, parts, paired, pairs_of_groups, sources, _ = laid_ref.shape
    slices = bins // (parts * LANES)
    steps = chunks // slices * paired
    half = sources // 2
    block = lax.broadcasted_iota(jnp.int32, (sources, LANES), 1) // run

    def chunk_step(q, carry):
        at = pl.ds(pl.multiple_of(q * LANES, LANES), LANES)
        for step in range(steps):
            first = pl.ds(pl.multiple_of(blocks_ref[step] * sources, sources), sources)
            tiles = [
                spectra_ref[i // 2, i % 2, first, at].astype(jnp.float32) for i in range(terms)
            ]
            gap = terms // 2
            while gap:
                high = (block // gap) % 2 == 1
                for i in range(terms):
                    if (i // gap) % 2 == 0:
                        low_tile, high_tile = tiles[i], tiles[i + gap]
                        tiles[i] = jnp.where(
                            high, pltpu.roll(high_tile, gap * run, 1), low_tile
                        )
                        tiles[i + gap] = jnp.where(
                            high, high_tile, pltpu.roll(low_tile, LANES - gap * run, 1)
                        )
                gap //= 2
            wide = [jnp.concatenate([tile[:half], tile[half:]], 1) for tile in tiles]
            chunk = step // paired * slices + q // parts
            for i in range(pairs_of_groups):
                laid_ref[chunk, q % parts, step % paired, i] = jnp.concatenate(
                    wide[2 * i : 2 * i + 2], 0
                ).astype(jnp.bfloat16)
        return carry

    lax.fori_loop(0, bins // LANES, chunk_step, 0)


def prepare(spectra, blocks, steps, sources, run):
    bins = spectra.shape[3]
    return pl.pallas_call(
        functools.partial(prepare_kernel, run=run),
        out_shape=jax.ShapeDtypeStruct(
            (steps // PAIRED * (bins // (PARTS * LANES)), PARTS, PAIRED)
            + (LANES // run // 2, sources, 2 * LANES),
            spectra.dtype,
        ),
        in_specs=[
            pl.BlockSpec(memory_space=pltpu.SMEM),
            pl.BlockSpec(memory_space=pltpu.VMEM),
        ],
        out_specs=pl.BlockSpec(memory_space=pltpu.VMEM),
        compiler_params=pltpu.CompilerParams(vmem_limit_bytes=16 << 20),
    )(blocks, spectra)


def main_kernel(
    owners_ref, own_ref, spectra_ref, lag_ref, out_ref,
    weights, cross_spectra, made, arrived, got,
    total_lags, sent, from_core, half, from_cross, quarter, from_low, from_high, to_high, to_low,
    core_send, core_recv, cross_send, cross_recv, up_send, up_recv,
    down_send, down_recv, share_send, share_recv, last_send, last_recv,
    sum_send, sum_recv,
    *, length, members, run,
):
    chunks, _, paired, groups, sources, width = own_ref.shape
    slices = lag_ref.shape[0]
    steps = chunks // slices * paired
    pairs = sources // 2
    windows, _, receivers, bins = spectra_ref.shape
    terms = 2 * windows
    kept = sources // members
    me = lax.axis_index("chan")
    win = lax.axis_index("win")
    line, cross, core = me // 4, (me // 2) % 2, me % 2
    core_peer = me + 1 - 2 * core
    cross_peer = me + 2 - 4 * cross
    mine = 2 * core + cross
    theirs = 2 * core + 1 - cross
    has_low, has_high = line > 0, line < length - 1
    near_low = line < length // 2

    def remote(src, dst, send, recv, peer):
        return pltpu.make_async_remote_copy(
            src_ref=src, dst_ref=dst, send_sem=send, recv_sem=recv,
            device_id={"chan": peer}, device_id_type=pl.DeviceIdType.MESH,
        )

    def to_core(s):
        part = own_ref.at[s, pl.ds(2 * (1 - core), 2)]
        return remote(part, from_core.at[s], core_send.at[s], core_recv.at[s], core_peer)

    def to_cross(s):
        return remote(
            half.at[s, 1 - cross], from_cross.at[s], cross_send.at[s], cross_recv.at[s],
            cross_peer,
        )

    def go_up(s):
        return remote(to_high.at[s], from_low.at[s], up_send.at[s], up_recv.at[s], me + 4)

    def go_down(s):
        return remote(to_low.at[s], from_high.at[s], down_send.at[s], down_recv.at[s], me - 4)

    def share(s):
        ref = got.at[s, mine]
        return remote(ref, ref, share_send.at[s], share_recv.at[s], cross_peer)

    def last(s, which, index):
        ref = got.at[s, index]
        return remote(ref, ref, last_send.at[s, which], last_recv.at[s, which], core_peer)

    def add_up(s, j):
        peer = (win + j) % members
        return pltpu.make_async_remote_copy(
            src_ref=sent.at[s, pl.ds(peer * kept, kept)],
            dst_ref=arrived.at[s, j - 1],
            send_sem=sum_send.at[s, j - 1],
            recv_sem=sum_recv.at[s, j - 1],
            device_id={"win": peer},
            device_id_type=pl.DeviceIdType.MESH,
        )

    barrier = pltpu.get_barrier_semaphore()

    def greet(peer):
        pl.semaphore_signal(
            barrier, inc=1, device_id={"chan": peer}, device_id_type=pl.DeviceIdType.MESH
        )

    greet(core_peer)
    greet(cross_peer)
    for j in range(1, members):
        pl.semaphore_signal(
            barrier,
            inc=1,
            device_id={"win": (win + j) % members},
            device_id_type=pl.DeviceIdType.MESH,
        )

    @pl.when(has_low)
    def _():
        greet(me - 4)

    @pl.when(has_high)
    def _():
        greet(me + 4)

    pl.semaphore_wait(
        barrier, 1 + members + jnp.where(has_low, 1, 0) + jnp.where(has_high, 1, 0)
    )

    def choose(ref, s, mine_if, own, other):
        for i in range(paired):
            owner = owners_ref[s // slices * paired + i]
            ref[s, i] = lax.select(mine_if(owner), own[i], other[i])

    @pl.loop(0, chunks)
    def _(s):
        to_core(s).start()

    @pl.loop(0, chunks)
    def _(s):
        to_core(s).wait_recv()
        for i in range(paired):
            owner = owners_ref[s // slices * paired + i]
            for k in range(2):
                half[s, k, i] = lax.select(
                    owner == me, own_ref[s, 2 * core + k, i], from_core[s, k, i]
                )

        @pl.when(s < 2)
        def _():
            to_cross(s).start()

    low_lanes = lax.broadcasted_iota(jnp.int32, (LANES, LANES), 1) < receivers
    zero = jnp.zeros((LANES, LANES), jnp.float32)

    def weigh(b):
        @pl.loop(0, PARTS)
        def _(part):
            q = b * PARTS + part
            at = pl.ds(pl.multiple_of(q * LANES, LANES), LANES)
            for w in range(windows):
                real = spectra_ref[w, 0, :, at].astype(jnp.float32)
                imag = spectra_ref[w, 1, :, at].astype(jnp.float32)
                both = jnp.concatenate([real, imag], 0).T
                swap = pltpu.roll(both, receivers, 1)
                real_low = jnp.where(low_lanes, both, zero)
                imag_high = jnp.where(low_lanes, zero, both)
                imag_low = jnp.where(low_lanes, swap, zero)
                real_high = jnp.where(low_lanes, zero, swap)
                for k, tile in enumerate(
                    (
                        jnp.concatenate([real_low, -imag_low], 1),
                        jnp.concatenate([imag_low, real_low], 1),
                        jnp.concatenate([real_high, -imag_high], 1),
                        jnp.concatenate([imag_high, real_high], 1),
                    )
                ):
                    tile = tile.astype(jnp.bfloat16)
                    row = (k // 2) * LANES + (2 * w + k % 2) * run
                    for g in range(2 * groups):
                        weights[q * 2 * groups + g, row : row + run] = tile[
                            g * run : (g + 1) * run
                        ]

    lane = lax.broadcasted_iota(jnp.int32, (run, width), 1) % run
    row = lax.broadcasted_iota(jnp.int32, (run, width), 0)
    keep = (lane == row).astype(jnp.float32)

    def cross_part(s, part):
        first = (s % slices * PARTS + part) * 2 * groups
        for g in range(groups):
            values = [got[s, part, i, g].astype(jnp.float32) for i in range(paired)]
            for e in range(2):
                rows = jnp.concatenate(
                    [
                        (jnp.broadcast_to(value[r : r + 1], (run, width)) * keep).astype(
                            jnp.bfloat16
                        )
                        for value in values
                        for r in range(e * pairs, (e + 1) * pairs)
                    ],
                    0,
                )
                dots = jnp.dot(
                    rows, weights[first + 2 * g + e], preferred_element_type=jnp.float32
                ).astype(jnp.bfloat16)
                base = pl.multiple_of((part * 2 * groups + 2 * g + e) * run, run)
                for i in range(paired):
                    for p in range(pairs):
                        one = dots[(i * pairs + p) * run : (i * pairs + p + 1) * run]
                        at = slice(p * LANES, (p + 1) * LANES)
                        cross_spectra[s % 2, i, 0, pl.ds(base, run), at] = one[:, :LANES]
                        cross_spectra[s % 2, i, 1, pl.ds(base, run), at] = one[:, LANES:]

    def lag_part(s):
        b = s % slices
        step = s // slices * paired

        @pl.when(b == 0)
        def _():
            total_lags[...] = jnp.zeros_like(total_lags)

        for i in range(paired):
            for n in range(pairs // 2):
                at = slice(n * 2 * LANES, (n + 1) * 2 * LANES)
                values = jnp.concatenate(
                    [cross_spectra[s % 2, i, 0, :, at], cross_spectra[s % 2, i, 1, :, at]], 0
                )
                total_lags[i, :, at] += jnp.dot(
                    lag_ref[b], values, preferred_element_type=jnp.float32
                )

            @pl.when(b == slices - 1)
            def _():
                for n in range(pairs // 2):
                    turned = total_lags[i, :, n * 2 * LANES : (n + 1) * 2 * LANES].T
                    for k in range(4):
                        source = 2 * n + k // 2 + (k % 2) * pairs
                        one = turned[k * receivers : (k + 1) * receivers]
                        made[step + i, source] = one
                        sent[step + i, source] = one.astype(jnp.bfloat16)
                for j in range(1, members):
                    add_up(step + i, j).start()

    def low_side(s):
        @pl.when(has_low)
        def _():
            go_up(s).wait_recv()
            choose(to_high, s, lambda o: o // 4 == line, quarter[s], from_low[s])

            @pl.when(has_high)
            def _():
                go_up(s).start()

    def high_side(s):
        @pl.when(has_high)
        def _():
            go_down(s).wait_recv()
            choose(to_low, s, lambda o: o // 4 == line, quarter[s], from_high[s])

            @pl.when(has_low)
            def _():
                go_down(s).start()

    def enter(s):
        to_cross(s).wait_recv()

        @pl.when(s + 2 < chunks)
        def _():
            to_cross(s + 2).start()

        choose(quarter, s, lambda o: (o // 2) % 2 == cross, half[s, cross], from_cross[s])

        @pl.when(line == 0)
        def _():
            to_high[s] = quarter[s]
            go_up(s).start()

        @pl.when(line == length - 1)
        def _():
            to_low[s] = quarter[s]
            go_down(s).start()

    def near_side(s):
        @pl.when(near_low)
        def _():
            low_side(s)

        @pl.when(jnp.logical_not(near_low))
        def _():
            high_side(s)

    def far_side(s):
        @pl.when(near_low)
        def _():
            high_side(s)

        @pl.when(jnp.logical_not(near_low))
        def _():
            low_side(s)

    inner = (line > 0) & (line < length - 1)

    def settle(s):
        @pl.when(jnp.logical_not(inner))
        def _():
            far_side(s)

        choose(got.at[:, mine], s, lambda o: o // 4 <= line, to_high[s], to_low[s])
        share(s).start()
        last(s, 0, mine).start()

    def pass_on(s):
        share(s).wait_recv()
        last(s, 1, theirs).start()

    @pl.loop(0, chunks + 4)
    def _(t):
        @pl.when(t >= 4)
        def _():
            pass_on(t - 4)

        @pl.when((t >= 3) & (t < chunks + 3))
        def _():
            settle(t - 3)

        @pl.when((t >= 2) & (t < chunks + 2) & inner)
        def _():
            far_side(t - 2)

        @pl.when((t >= 1) & (t < chunks + 1))
        def _():
            near_side(t - 1)

        @pl.when(t < chunks)
        def _():
            enter(t)

        @pl.when(t < slices)
        def _():
            weigh(t)

        @pl.when((t >= 3) & (t < chunks + 3))
        def _():
            cross_part(t - 3, mine)

        @pl.when(t >= 4)
        def _():
            s = t - 4
            cross_part(s, theirs)
            for which in range(2):
                last(s, which, mine).wait_recv()
            cross_part(s, 2 * (1 - core))
            cross_part(s, 2 * (1 - core) + 1)
            lag_part(s)

    @pl.loop(0, chunks)
    def _(s):
        to_core(s).wait_send()
        to_cross(s).wait_send()
        share(s).wait_send()
        for which in range(2):
            last(s, which, mine).wait_send()

        @pl.when(has_high)
        def _():
            go_up(s).wait_send()

        @pl.when(has_low)
        def _():
            go_down(s).wait_send()

    @pl.loop(0, steps)
    def _(s):
        total = made[s, pl.ds(win * kept, kept)]
        for j in range(1, members):
            add_up(s, j).wait()
            total += arrived[s, j - 1].astype(jnp.float32)
        out_ref[s] = total


def main(laid, spectra, table, owners, run):
    chunks, _, paired, groups, sources, width = laid.shape
    windows, _, receivers, bins = spectra.shape
    members = lax.axis_size("win")
    slices, lags, depth = table.shape
    steps = chunks // slices * paired
    dtype = laid.dtype
    piece = (paired, groups, sources, width)
    kept = (sources // members, receivers, lags)
    return pl.pallas_call(
        functools.partial(
            main_kernel, length=lax.axis_size("chan") // 4, members=members, run=run
        ),
        out_shape=jax.ShapeDtypeStruct((steps,) + kept, jnp.float32),
        in_specs=[pl.BlockSpec(memory_space=pltpu.SMEM)]
        + [pl.BlockSpec(memory_space=pltpu.VMEM)] * 3,
        out_specs=pl.BlockSpec(memory_space=pltpu.VMEM),
        scratch_shapes=[
            pltpu.VMEM((bins // run, 2 * LANES, 2 * LANES), dtype),
            pltpu.VMEM((2, paired, 2, bins // slices, sources // 2 * LANES), dtype),
            pltpu.VMEM((steps, sources, receivers, lags), jnp.float32),
            pltpu.VMEM((steps, members - 1) + kept, dtype),
            pltpu.VMEM((chunks, PARTS) + piece, dtype),
            pltpu.VMEM((paired, lags, sources // 2 * LANES), jnp.float32),
            pltpu.VMEM((steps, sources, receivers, lags), dtype),
            pltpu.VMEM((chunks, 2) + piece, dtype),
            pltpu.VMEM((chunks, 2) + piece, dtype),
        ]
        + [pltpu.VMEM((chunks,) + piece, dtype)] * 6
        + [pltpu.SemaphoreType.DMA((chunks,))] * 10
        + [pltpu.SemaphoreType.DMA((chunks, 2))] * 2
        + [pltpu.SemaphoreType.DMA((steps, members - 1))] * 2,
        compiler_params=pltpu.CompilerParams(
            collective_id=0, has_side_effects=True, vmem_limit_bytes=60 << 20
        ),
    )(owners, laid, spectra, table)


def body(spectra, owners, blocks, max_lag):
    window_count, _, _, bin_count = spectra.shape
    group_count = lax.axis_size("win")
    run = LANES // (2 * window_count)
    slices = bin_count // (PARTS * LANES)
    table = jnp.asarray(lag_rows(bin_count, LAGS, window_count * group_count, slices))
    turned = spectra.transpose(0, 2, 1, 3)
    laid = prepare(turned, blocks, STEPS, SRC, run)
    stacked = main(laid, turned, table, owners, run)
    offsets = jnp.abs(jnp.arange(LAGS, dtype=jnp.int32) - LAGS // 2)
    inside = offsets[None, None, None, :] <= max_lag[:, :, :, None]
    return jnp.where(inside, stacked, jnp.float32(0.0))


def solution(mesh):
    return jax.shard_map(
        body,
        mesh=mesh,
        in_specs=(P("win", "chan", None, None), P(), P(), P(None, "win", "chan")),
        out_specs=P(None, "win", "chan", None),
        check_vma=False,
    )
```

```python
import functools

import jax
import jax.numpy as jnp
import numpy as np
from jax import lax
from jax.experimental import pallas as pl
from jax.experimental.pallas import tpu as pltpu
from jax.sharding import PartitionSpec as P

SRC = 16
STEPS = 4
LAGS = 128
LANES = 128
PARTS = 4
PAIRED = 2


def lag_rows(bin_count, lag_count, window_count, slices):
    bins = np.arange(bin_count, dtype=np.int64)[None, :]
    offsets = np.arange(lag_count, dtype=np.int64)[:, None] - lag_count // 2
    phase = (bins * offsets % (2 * bin_count)) * (np.pi / bin_count)
    weight = np.where(bins == 0, 1.0, 2.0) / np.sqrt(2.0 * bin_count * window_count)
    rows = np.stack([weight * np.cos(phase), -weight * np.sin(phase)], 1)
    rows = rows.reshape(lag_count, 2, slices, bin_count // slices).transpose(2, 0, 1, 3)
    return rows.reshape(slices, lag_count, -1).astype(np.float32).astype(jnp.bfloat16)


def main_kernel(
    owners_ref, blocks_ref, spectra_ref, lag_ref, out_ref,
    own, weights, cross_spectra, made, arrived, got,
    sent, from_core, half, from_cross, quarter, from_low, from_high, to_high, to_low,
    core_send, core_recv, cross_send, cross_recv, up_send, up_recv,
    down_send, down_recv, share_send, share_recv, last_send, last_recv,
    sum_send, sum_recv,
    *, length, members, run,
):
    chunks, parts, paired, groups, sources, width = own.shape
    slices = lag_ref.shape[0]
    steps = chunks // slices * paired
    pairs = sources // 2
    windows, _, receivers, bins = spectra_ref.shape
    terms = 2 * windows
    kept = sources // members
    me = lax.axis_index("chan")
    win = lax.axis_index("win")
    line, cross, core = me // 4, (me // 2) % 2, me % 2
    core_peer = me + 1 - 2 * core
    cross_peer = me + 2 - 4 * cross
    mine = 2 * core + cross
    theirs = 2 * core + 1 - cross
    has_low, has_high = line > 0, line < length - 1
    near_low = line < length // 2

    def remote(src, dst, send, recv, peer):
        return pltpu.make_async_remote_copy(
            src_ref=src, dst_ref=dst, send_sem=send, recv_sem=recv,
            device_id={"chan": peer}, device_id_type=pl.DeviceIdType.MESH,
        )

    def to_core(s):
        part = own.at[s, pl.ds(2 * (1 - core), 2)]
        return remote(part, from_core.at[s], core_send.at[s], core_recv.at[s], core_peer)

    def to_cross(s):
        return remote(
            half.at[s, 1 - cross], from_cross.at[s], cross_send.at[s], cross_recv.at[s],
            cross_peer,
        )

    def go_up(s):
        return remote(to_high.at[s], from_low.at[s], up_send.at[s], up_recv.at[s], me + 4)

    def go_down(s):
        return remote(to_low.at[s], from_high.at[s], down_send.at[s], down_recv.at[s], me - 4)

    def share(s):
        ref = got.at[s, mine]
        return remote(ref, ref, share_send.at[s], share_recv.at[s], cross_peer)

    def last(s, which, index):
        ref = got.at[s, index]
        return remote(ref, ref, last_send.at[s, which], last_recv.at[s, which], core_peer)

    def add_up(s, j):
        peer = (win + j) % members
        return pltpu.make_async_remote_copy(
            src_ref=sent.at[s, pl.ds(peer * kept, kept)],
            dst_ref=arrived.at[s, j - 1],
            send_sem=sum_send.at[s, j - 1],
            recv_sem=sum_recv.at[s, j - 1],
            device_id={"win": peer},
            device_id_type=pl.DeviceIdType.MESH,
        )

    barrier = pltpu.get_barrier_semaphore()

    def greet(peer):
        pl.semaphore_signal(
            barrier, inc=1, device_id={"chan": peer}, device_id_type=pl.DeviceIdType.MESH
        )

    greet(core_peer)
    greet(cross_peer)
    for j in range(1, members):
        pl.semaphore_signal(
            barrier,
            inc=1,
            device_id={"win": (win + j) % members},
            device_id_type=pl.DeviceIdType.MESH,
        )

    @pl.when(has_low)
    def _():
        greet(me - 4)

    @pl.when(has_high)
    def _():
        greet(me + 4)

    pl.semaphore_wait(
        barrier, 1 + members + jnp.where(has_low, 1, 0) + jnp.where(has_high, 1, 0)
    )

    def choose(ref, s, mine_if, own, other):
        for i in range(paired):
            owner = owners_ref[s // slices * paired + i]
            ref[s, i] = lax.select(mine_if(owner), own[i], other[i])

    block = lax.broadcasted_iota(jnp.int32, (sources, LANES), 1) // run
    odd = [(block // bit) % 2 == 1 for bit in (1, 2, 4)]

    def lay(s):
        @pl.loop(0, parts)
        def _(part):
            q = s % slices * parts + part
            at = pl.ds(pl.multiple_of(q * LANES, LANES), LANES)
            for j in range(paired):
                place = blocks_ref[s // slices * paired + j]
                tiles = []
                for i in range(terms):
                    tile = spectra_ref[i // 2, i % 2, :sources, at]
                    for k in range(1, receivers // sources):
                        here = spectra_ref[i // 2, i % 2, k * sources : (k + 1) * sources, at]
                        tile = lax.select(place == k, here, tile)
                    tiles.append(tile.astype(jnp.float32))
                tiles = [tiles[0]] + [pltpu.roll(tiles[i], i * run, 1) for i in range(1, terms)]
                for k, mask in enumerate(odd):
                    tiles = [
                        jnp.where(mask, tiles[(i + (1 << k)) % terms], tiles[i])
                        for i in range(terms)
                    ]
                wide = [
                    jnp.concatenate([tiles[-g % terms][:pairs], tiles[-g % terms][pairs:]], 1)
                    for g in range(2 * groups)
                ]
                for g in range(groups):
                    own[s, part, j, g] = jnp.concatenate(
                        wide[2 * g : 2 * g + 2], 0
                    ).astype(jnp.bfloat16)

    def leave(s):
        to_core(s).wait_recv()
        for i in range(paired):
            owner = owners_ref[s // slices * paired + i]
            for k in range(2):
                half[s, k, i] = lax.select(
                    owner == me, own[s, 2 * core + k, i], from_core[s, k, i]
                )
        to_cross(s).start()

    @pl.loop(0, chunks + 2)
    def _(t):
        @pl.when(t < chunks)
        def _():
            lay(t)
            to_core(t).start()

        @pl.when(t >= 2)
        def _():
            leave(t - 2)

    low_lanes = lax.broadcasted_iota(jnp.int32, (LANES, LANES), 1) < receivers
    zero = jnp.zeros((LANES, LANES), jnp.float32)

    def weigh(b):
        @pl.loop(0, PARTS)
        def _(part):
            q = b * PARTS + part
            at = pl.ds(pl.multiple_of(q * LANES, LANES), LANES)
            for w in range(windows):
                real = spectra_ref[w, 0, :, at].astype(jnp.float32)
                imag = spectra_ref[w, 1, :, at].astype(jnp.float32)
                both = jnp.concatenate([real, imag], 0).T
                swap = pltpu.roll(both, receivers, 1)
                real_low = jnp.where(low_lanes, both, zero)
                imag_high = jnp.where(low_lanes, zero, both)
                imag_low = jnp.where(low_lanes, swap, zero)
                real_high = jnp.where(low_lanes, zero, swap)
                for k, tile in enumerate(
                    (
                        jnp.concatenate([real_low, -imag_low], 1),
                        jnp.concatenate([imag_low, real_low], 1),
                        jnp.concatenate([real_high, -imag_high], 1),
                        jnp.concatenate([imag_high, real_high], 1),
                    )
                ):
                    tile = tile.astype(jnp.bfloat16)
                    for g in range(2 * groups):
                        row = (k // 2) * LANES + (2 * w + k % 2 + g) % terms * run
                        weights[q * 2 * groups + g, row : row + run] = tile[
                            g * run : (g + 1) * run
                        ]

    lane = lax.broadcasted_iota(jnp.int32, (run, width), 1) % run
    row = lax.broadcasted_iota(jnp.int32, (run, width), 0)
    keep = (lane == row).astype(jnp.float32)

    def cross_part(s, part):
        first = (s % slices * PARTS + part) * 2 * groups
        for g in range(groups):
            values = [got[s, part, i, g].astype(jnp.float32) for i in range(paired)]
            for e in range(2):
                rows = jnp.concatenate(
                    [
                        (jnp.broadcast_to(value[r : r + 1], (run, width)) * keep).astype(
                            jnp.bfloat16
                        )
                        for value in values
                        for r in range(e * pairs, (e + 1) * pairs)
                    ],
                    0,
                )
                dots = jnp.dot(
                    rows, weights[first + 2 * g + e], preferred_element_type=jnp.float32
                ).astype(jnp.bfloat16)
                base = pl.multiple_of((part * 2 * groups + 2 * g + e) * run, run)
                for i in range(paired):
                    for p in range(pairs):
                        one = dots[(i * pairs + p) * run : (i * pairs + p + 1) * run]
                        at = slice(p * LANES, (p + 1) * LANES)
                        cross_spectra[i, s % slices, 0, pl.ds(base, run), at] = one[:, :LANES]
                        cross_spectra[i, s % slices, 1, pl.ds(base, run), at] = one[:, LANES:]

    def lag_part(s, last_one):
        b = s % slices
        step = s // slices * paired
        for i in range(paired):
            for n in range(pairs // 2):
                at = slice(n * 2 * LANES, (n + 1) * 2 * LANES)
                values = jnp.concatenate(
                    [cross_spectra[i, b - 1 + k // 2, k % 2, :, at] for k in range(4)], 0
                )
                table = jnp.concatenate([lag_ref[b - 1], lag_ref[b]], 1)
                turned = jnp.dot(table, values, preferred_element_type=jnp.float32).T
                for k in range(4):
                    source = 2 * n + k // 2 + (k % 2) * pairs
                    one = turned[k * receivers : (k + 1) * receivers]
                    if not last_one:
                        made[step + i, source] = one
                        continue
                    one += made[step + i, source]
                    made[step + i, source] = one
                    sent[step + i, source] = one.astype(jnp.bfloat16)
            if last_one:
                for j in range(1, members):
                    add_up(step + i, j).start()

    def low_side(s):
        @pl.when(has_low)
        def _():
            go_up(s).wait_recv()
            choose(to_high, s, lambda o: o // 4 == line, quarter[s], from_low[s])

            @pl.when(has_high)
            def _():
                go_up(s).start()

    def high_side(s):
        @pl.when(has_high)
        def _():
            go_down(s).wait_recv()
            choose(to_low, s, lambda o: o // 4 == line, quarter[s], from_high[s])

            @pl.when(has_low)
            def _():
                go_down(s).start()

    def enter(s):
        to_cross(s).wait_recv()

        choose(quarter, s, lambda o: (o // 2) % 2 == cross, half[s, cross], from_cross[s])

        @pl.when(line == 0)
        def _():
            to_high[s] = quarter[s]
            go_up(s).start()

        @pl.when(line == length - 1)
        def _():
            to_low[s] = quarter[s]
            go_down(s).start()

    def near_side(s):
        @pl.when(near_low)
        def _():
            low_side(s)

        @pl.when(jnp.logical_not(near_low))
        def _():
            high_side(s)

    def far_side(s):
        @pl.when(near_low)
        def _():
            high_side(s)

        @pl.when(jnp.logical_not(near_low))
        def _():
            low_side(s)

    inner = (line > 0) & (line < length - 1)

    def settle(s):
        @pl.when(jnp.logical_not(inner))
        def _():
            far_side(s)

        choose(got.at[:, mine], s, lambda o: o // 4 <= line, to_high[s], to_low[s])
        share(s).start()
        last(s, 0, mine).start()

    def pass_on(s):
        share(s).wait_recv()
        last(s, 1, theirs).start()

    def at(t, delay):
        return (t >= delay) & (t < chunks + delay)

    @pl.loop(0, chunks + 8)
    def _(t):
        @pl.when(t < chunks)
        def _():
            enter(t)

        @pl.when(at(t, 2))
        def _():
            near_side(t - 2)

        @pl.when(at(t, 4) & inner)
        def _():
            far_side(t - 4)

        @pl.when(at(t, 6))
        def _():
            settle(t - 6)

        @pl.when(t >= 8)
        def _():
            pass_on(t - 8)

        @pl.when(t < slices)
        def _():
            weigh(t)

        @pl.when(at(t, 6))
        def _():
            cross_part(t - 6, mine)

        @pl.when(t >= 8)
        def _():
            s = t - 8
            cross_part(s, theirs)
            for which in range(2):
                last(s, which, mine).wait_recv()
            cross_part(s, 2 * (1 - core))
            cross_part(s, 2 * (1 - core) + 1)

            @pl.when(s % slices == slices // 2 - 1)
            def _():
                lag_part(s, False)

            @pl.when(s % slices == slices - 1)
            def _():
                lag_part(s, True)

    @pl.loop(0, chunks)
    def _(s):
        to_core(s).wait_send()
        to_cross(s).wait_send()
        share(s).wait_send()
        for which in range(2):
            last(s, which, mine).wait_send()

        @pl.when(has_high)
        def _():
            go_up(s).wait_send()

        @pl.when(has_low)
        def _():
            go_down(s).wait_send()

    @pl.loop(0, steps)
    def _(s):
        total = made[s, pl.ds(win * kept, kept)]
        for j in range(1, members):
            add_up(s, j).wait()
            total += arrived[s, j - 1].astype(jnp.float32)
        out_ref[s] = total


def main(spectra, table, owners, blocks, run):
    windows, _, receivers, bins = spectra.shape
    members = lax.axis_size("win")
    slices, lags, _ = table.shape
    steps, sources, dtype = STEPS, SRC, spectra.dtype
    chunks = steps // PAIRED * slices
    piece = (PAIRED, LANES // run // 2, sources, 2 * LANES)
    kept = (sources // members, receivers, lags)
    return pl.pallas_call(
        functools.partial(
            main_kernel, length=lax.axis_size("chan") // 4, members=members, run=run
        ),
        out_shape=jax.ShapeDtypeStruct((steps,) + kept, jnp.float32),
        in_specs=[pl.BlockSpec(memory_space=pltpu.SMEM)] * 2
        + [pl.BlockSpec(memory_space=pltpu.VMEM)] * 2,
        out_specs=pl.BlockSpec(memory_space=pltpu.VMEM),
        scratch_shapes=[
            pltpu.VMEM((chunks, PARTS) + piece, dtype),
            pltpu.VMEM((bins // run, 2 * LANES, 2 * LANES), dtype),
            pltpu.VMEM((PAIRED, slices, 2, bins // slices, sources // 2 * LANES), dtype),
            pltpu.VMEM((steps, sources, receivers, lags), jnp.float32),
            pltpu.VMEM((steps, members - 1) + kept, dtype),
            pltpu.VMEM((chunks, PARTS) + piece, dtype),
            pltpu.VMEM((steps, sources, receivers, lags), dtype),
            pltpu.VMEM((chunks, 2) + piece, dtype),
            pltpu.VMEM((chunks, 2) + piece, dtype),
        ]
        + [pltpu.VMEM((chunks,) + piece, dtype)] * 6
        + [pltpu.SemaphoreType.DMA((chunks,))] * 10
        + [pltpu.SemaphoreType.DMA((chunks, 2))] * 2
        + [pltpu.SemaphoreType.DMA((steps, members - 1))] * 2,
        compiler_params=pltpu.CompilerParams(
            collective_id=0, has_side_effects=True, vmem_limit_bytes=60 << 20
        ),
    )(owners, blocks, spectra, table)


def body(spectra, owners, blocks, max_lag):
    window_count, _, _, bin_count = spectra.shape
    group_count = lax.axis_size("win")
    run = LANES // (2 * window_count)
    slices = bin_count // (PARTS * LANES)
    table = jnp.asarray(lag_rows(bin_count, LAGS, window_count * group_count, slices))
    turned = spectra.transpose(0, 2, 1, 3)
    stacked = main(turned, table, owners, blocks, run)
    offsets = jnp.abs(jnp.arange(LAGS, dtype=jnp.int32) - LAGS // 2)
    inside = offsets[None, None, None, :] <= max_lag[:, :, :, None]
    return jnp.where(inside, stacked, jnp.float32(0.0))


def solution(mesh):
    return jax.shard_map(
        body,
        mesh=mesh,
        in_specs=(P("win", "chan", None, None), P(), P(), P(None, "win", "chan")),
        out_specs=P(None, "win", "chan", None),
        check_vma=False,
    )
```

```python
import functools

import jax
import jax.numpy as jnp
import numpy as np
from jax import lax
from jax.experimental import pallas as pl
from jax.experimental.pallas import tpu as pltpu
from jax.sharding import PartitionSpec as P

SRC = 16
STEPS = 4
LAGS = 128
LANES = 128
PARTS = 4
PAIRED = 2


def lag_rows(bin_count, lag_count, window_count, slices):
    bins = np.arange(bin_count, dtype=np.int64)[None, :]
    offsets = np.arange(lag_count, dtype=np.int64)[:, None] - lag_count // 2
    phase = (bins * offsets % (2 * bin_count)) * (np.pi / bin_count)
    weight = np.where(bins == 0, 1.0, 2.0) / np.sqrt(2.0 * bin_count * window_count)
    rows = np.stack([weight * np.cos(phase), -weight * np.sin(phase)], 1)
    rows = rows.reshape(lag_count, 2, slices, bin_count // slices).transpose(2, 0, 1, 3)
    return rows.reshape(slices, lag_count, -1).astype(np.float32).astype(jnp.bfloat16)


def placement(receivers):
    places = np.zeros((2, 2, 2 * receivers, 4, receivers), np.float32)
    c = np.arange(receivers)
    for half in range(2):
        places[half, 0, 2 * c, half, c] = 1
        places[half, 0, 2 * c + 1, 2 + half, c] = -1
        places[half, 1, 2 * c + 1, half, c] = 1
        places[half, 1, 2 * c, 2 + half, c] = 1
    return places.reshape(4, 2 * receivers, 4 * receivers).astype(jnp.bfloat16)


def main_kernel(
    owners_ref, blocks_ref, spectra_ref, lag_ref, place_ref, limit_ref, out_ref,
    own, weights, cross_spectra, made, arrived, got,
    sent, from_core, half, from_cross, quarter, from_low, from_high, to_high, to_low,
    core_send, core_recv, cross_send, cross_recv, up_send, up_recv,
    down_send, down_recv, share_send, share_recv, last_send, last_recv,
    sum_send, sum_recv,
    *, length, members, run,
):
    chunks, parts, paired, groups, sources, width = own.shape
    slices = lag_ref.shape[0]
    steps = chunks // slices * paired
    pairs = sources // 2
    windows, receivers, _, bins = spectra_ref.shape
    terms = 2 * windows
    kept = sources // members
    me = lax.axis_index("chan")
    win = lax.axis_index("win")
    line, cross, core = me // 4, (me // 2) % 2, me % 2
    core_peer = me + 1 - 2 * core
    cross_peer = me + 2 - 4 * cross
    mine = 2 * core + cross
    theirs = 2 * core + 1 - cross
    has_low, has_high = line > 0, line < length - 1
    near_low = line < length // 2

    def remote(src, dst, send, recv, peer):
        return pltpu.make_async_remote_copy(
            src_ref=src, dst_ref=dst, send_sem=send, recv_sem=recv,
            device_id={"chan": peer}, device_id_type=pl.DeviceIdType.MESH,
        )

    def to_core(s):
        part = own.at[s, pl.ds(2 * (1 - core), 2)]
        return remote(part, from_core.at[s], core_send.at[s], core_recv.at[s], core_peer)

    def to_cross(s):
        return remote(
            half.at[s, 1 - cross], from_cross.at[s], cross_send.at[s], cross_recv.at[s],
            cross_peer,
        )

    def go_up(s):
        return remote(to_high.at[s], from_low.at[s], up_send.at[s], up_recv.at[s], me + 4)

    def go_down(s):
        return remote(to_low.at[s], from_high.at[s], down_send.at[s], down_recv.at[s], me - 4)

    def share(s):
        ref = got.at[s, mine]
        return remote(ref, ref, share_send.at[s], share_recv.at[s], cross_peer)

    def last(s, which, index):
        ref = got.at[s, index]
        return remote(ref, ref, last_send.at[s, which], last_recv.at[s, which], core_peer)

    def add_up(s, j):
        peer = (win + j) % members
        return pltpu.make_async_remote_copy(
            src_ref=sent.at[s, pl.ds(peer * kept, kept)],
            dst_ref=arrived.at[s, j - 1],
            send_sem=sum_send.at[s, j - 1],
            recv_sem=sum_recv.at[s, j - 1],
            device_id={"win": peer},
            device_id_type=pl.DeviceIdType.MESH,
        )

    barrier = pltpu.get_barrier_semaphore()

    def greet(peer):
        pl.semaphore_signal(
            barrier, inc=1, device_id={"chan": peer}, device_id_type=pl.DeviceIdType.MESH
        )

    greet(core_peer)
    greet(cross_peer)
    for j in range(1, members):
        pl.semaphore_signal(
            barrier,
            inc=1,
            device_id={"win": (win + j) % members},
            device_id_type=pl.DeviceIdType.MESH,
        )

    @pl.when(has_low)
    def _():
        greet(me - 4)

    @pl.when(has_high)
    def _():
        greet(me + 4)

    pl.semaphore_wait(
        barrier, 1 + members + jnp.where(has_low, 1, 0) + jnp.where(has_high, 1, 0)
    )

    def choose(ref, s, mine_if, own, other):
        for i in range(paired):
            owner = owners_ref[s // slices * paired + i]
            ref[s, i] = lax.select(mine_if(owner), own[i], other[i])

    block = lax.broadcasted_iota(jnp.int32, (sources, LANES), 1) // run
    odd = [(block // bit) % 2 == 1 for bit in (1, 2, 4)]

    def choice(s):
        shape = (2 * paired * sources, 2 * receivers)
        row = lax.broadcasted_iota(jnp.int32, shape, 0)
        column = lax.broadcasted_iota(jnp.int32, shape, 1)
        first = s // slices * paired
        place = jnp.full(shape, blocks_ref[first], jnp.int32)
        for j in range(1, paired):
            place = jnp.where(row < 2 * sources * j, place, blocks_ref[first + j])
        wanted = 2 * (place * sources + row % sources) + row // sources % 2
        return jnp.where(column == wanted, 1.0, 0.0).astype(jnp.bfloat16)

    def channels(w, at, size):
        return spectra_ref[w, :, :, at].reshape(2 * receivers, size)

    def lay(s):
        picks = choice(s)

        @pl.loop(0, parts // 2)
        def _(two):
            q = s % slices * parts + 2 * two
            at = pl.ds(pl.multiple_of(q * LANES, 2 * LANES), 2 * LANES)
            found = [
                jnp.dot(picks, channels(w, at, 2 * LANES), preferred_element_type=jnp.float32)
                for w in range(windows)
            ]
            for e in range(2):
                for j in range(paired):
                    tiles = []
                    for i in range(terms):
                        top = (2 * j + i % 2) * sources
                        tile = found[i // 2][top : top + sources, e * LANES : (e + 1) * LANES]
                        tiles.append(pltpu.roll(tile, i * run, 1) if i else tile)
                    for k, mask in enumerate(odd):
                        tiles = [
                            jnp.where(mask, tiles[(i + (1 << k)) % terms], tiles[i])
                            for i in range(terms)
                        ]
                    wide = [
                        jnp.concatenate([tiles[-g % terms][:pairs], tiles[-g % terms][pairs:]], 1)
                        for g in range(2 * groups)
                    ]
                    for g in range(groups):
                        own[s, 2 * two + e, j, g] = jnp.concatenate(
                            wide[2 * g : 2 * g + 2], 0
                        ).astype(jnp.bfloat16)

    def leave(s):
        to_core(s).wait_recv()
        for i in range(paired):
            owner = owners_ref[s // slices * paired + i]
            for k in range(2):
                half[s, k, i] = lax.select(
                    owner == me, own[s, 2 * core + k, i], from_core[s, k, i]
                )
        to_cross(s).start()

    @pl.loop(0, chunks + 2)
    def _(t):
        @pl.when(t < chunks)
        def _():
            lay(t)
            to_core(t).start()

        @pl.when(t >= 2)
        def _():
            leave(t - 2)

    def weigh(b):
        @pl.loop(0, PARTS)
        def _(part):
            q = b * PARTS + part
            at = pl.ds(pl.multiple_of(q * LANES, LANES), LANES)
            for w in range(windows):
                turned = channels(w, at, LANES).T
                for k in range(4):
                    tile = jnp.dot(
                        turned, place_ref[k], preferred_element_type=jnp.float32
                    ).astype(jnp.bfloat16)
                    for g in range(2 * groups):
                        row = (k // 2) * LANES + (2 * w + k % 2 + g) % terms * run
                        weights[q * 2 * groups + g, row : row + run] = tile[
                            g * run : (g + 1) * run
                        ]

    def limits():
        same = lax.broadcasted_iota(jnp.int32, (receivers, receivers), 0) == (
            lax.broadcasted_iota(jnp.int32, (receivers, receivers), 1)
        )
        for s in range(steps):
            for k in range(kept):
                line_of = limit_ref[s, k : k + 1].astype(jnp.float32)
                column = jnp.where(same, jnp.broadcast_to(line_of, same.shape), 0.0)
                column = jnp.sum(column, axis=1, keepdims=True)
                out_ref[s, k] = jnp.broadcast_to(column, out_ref.shape[2:])

    lane = lax.broadcasted_iota(jnp.int32, (run, width), 1) % run
    row = lax.broadcasted_iota(jnp.int32, (run, width), 0)
    keep = (lane == row).astype(jnp.float32)

    def cross_part(s, part):
        first = (s % slices * PARTS + part) * 2 * groups
        for g in range(groups):
            values = [got[s, part, i, g].astype(jnp.float32) for i in range(paired)]
            for e in range(2):
                rows = jnp.concatenate(
                    [
                        (jnp.broadcast_to(value[r : r + 1], (run, width)) * keep).astype(
                            jnp.bfloat16
                        )
                        for value in values
                        for r in range(e * pairs, (e + 1) * pairs)
                    ],
                    0,
                )
                dots = jnp.dot(
                    rows, weights[first + 2 * g + e], preferred_element_type=jnp.float32
                ).astype(jnp.bfloat16)
                base = pl.multiple_of((part * 2 * groups + 2 * g + e) * run, run)
                for i in range(paired):
                    for p in range(pairs):
                        one = dots[(i * pairs + p) * run : (i * pairs + p + 1) * run]
                        at = slice(p * LANES, (p + 1) * LANES)
                        cross_spectra[i, s % slices, 0, pl.ds(base, run), at] = one[:, :LANES]
                        cross_spectra[i, s % slices, 1, pl.ds(base, run), at] = one[:, LANES:]

    def lag_part(s, last_one):
        b = s % slices
        step = s // slices * paired
        for i in range(paired):
            for n in range(pairs // 2):
                at = slice(n * 2 * LANES, (n + 1) * 2 * LANES)
                values = jnp.concatenate(
                    [cross_spectra[i, b - 1 + k // 2, k % 2, :, at] for k in range(4)], 0
                )
                table = jnp.concatenate([lag_ref[b - 1], lag_ref[b]], 1)
                turned = jnp.dot(table, values, preferred_element_type=jnp.float32).T
                for k in range(4):
                    source = 2 * n + k // 2 + (k % 2) * pairs
                    one = turned[k * receivers : (k + 1) * receivers]
                    if not last_one:
                        made[step + i, source] = one
                        continue
                    one += made[step + i, source]
                    made[step + i, source] = one
                    sent[step + i, source] = one.astype(jnp.bfloat16)
            if last_one:
                for j in range(1, members):
                    add_up(step + i, j).start()

    def low_side(s):
        @pl.when(has_low)
        def _():
            go_up(s).wait_recv()
            choose(to_high, s, lambda o: o // 4 == line, quarter[s], from_low[s])

            @pl.when(has_high)
            def _():
                go_up(s).start()

    def high_side(s):
        @pl.when(has_high)
        def _():
            go_down(s).wait_recv()
            choose(to_low, s, lambda o: o // 4 == line, quarter[s], from_high[s])

            @pl.when(has_low)
            def _():
                go_down(s).start()

    def enter(s):
        to_cross(s).wait_recv()

        choose(quarter, s, lambda o: (o // 2) % 2 == cross, half[s, cross], from_cross[s])

        @pl.when(line == 0)
        def _():
            to_high[s] = quarter[s]
            go_up(s).start()

        @pl.when(line == length - 1)
        def _():
            to_low[s] = quarter[s]
            go_down(s).start()

    def near_side(s):
        @pl.when(near_low)
        def _():
            low_side(s)

        @pl.when(jnp.logical_not(near_low))
        def _():
            high_side(s)

    def far_side(s):
        @pl.when(near_low)
        def _():
            high_side(s)

        @pl.when(jnp.logical_not(near_low))
        def _():
            low_side(s)

    inner = (line > 0) & (line < length - 1)

    def settle(s):
        @pl.when(jnp.logical_not(inner))
        def _():
            far_side(s)

        choose(got.at[:, mine], s, lambda o: o // 4 <= line, to_high[s], to_low[s])
        share(s).start()
        last(s, 0, mine).start()

    def pass_on(s):
        share(s).wait_recv()
        last(s, 1, theirs).start()

    limits()

    def at(t, delay):
        return (t >= delay) & (t < chunks + delay)

    @pl.loop(0, chunks + 8)
    def _(t):
        @pl.when(t < chunks)
        def _():
            enter(t)

        @pl.when(at(t, 2))
        def _():
            near_side(t - 2)

        @pl.when(at(t, 4) & inner)
        def _():
            far_side(t - 4)

        @pl.when(at(t, 6))
        def _():
            settle(t - 6)

        @pl.when(t >= 8)
        def _():
            pass_on(t - 8)

        @pl.when(t < slices)
        def _():
            weigh(t)

        @pl.when(at(t, 6))
        def _():
            cross_part(t - 6, mine)

        @pl.when(t >= 8)
        def _():
            s = t - 8
            cross_part(s, theirs)
            for which in range(2):
                last(s, which, mine).wait_recv()
            cross_part(s, 2 * (1 - core))
            cross_part(s, 2 * (1 - core) + 1)

            @pl.when(s % slices == slices // 2 - 1)
            def _():
                lag_part(s, False)

            @pl.when(s % slices == slices - 1)
            def _():
                lag_part(s, True)

    @pl.loop(0, chunks)
    def _(s):
        to_core(s).wait_send()
        to_cross(s).wait_send()
        share(s).wait_send()
        for which in range(2):
            last(s, which, mine).wait_send()

        @pl.when(has_high)
        def _():
            go_up(s).wait_send()

        @pl.when(has_low)
        def _():
            go_down(s).wait_send()

    @pl.loop(0, steps)
    def _(s):
        total = made[s, pl.ds(win * kept, kept)]
        for j in range(1, members):
            add_up(s, j).wait()
            total += arrived[s, j - 1].astype(jnp.float32)
        offset = lax.broadcasted_iota(jnp.int32, total.shape, 2) - total.shape[2] // 2
        inside = jnp.abs(offset).astype(jnp.float32) <= out_ref[s]
        out_ref[s] = jnp.where(inside, total, 0.0)


def main(spectra, table, places, owners, blocks, max_lag, run):
    windows, receivers, _, bins = spectra.shape
    members = lax.axis_size("win")
    slices, lags, _ = table.shape
    steps, sources, dtype = STEPS, SRC, spectra.dtype
    chunks = steps // PAIRED * slices
    piece = (PAIRED, LANES // run // 2, sources, 2 * LANES)
    kept = (sources // members, receivers, lags)
    return pl.pallas_call(
        functools.partial(
            main_kernel, length=lax.axis_size("chan") // 4, members=members, run=run
        ),
        out_shape=jax.ShapeDtypeStruct((steps,) + kept, jnp.float32),
        in_specs=[pl.BlockSpec(memory_space=pltpu.SMEM)] * 2
        + [pl.BlockSpec(memory_space=pltpu.VMEM)] * 4,
        out_specs=pl.BlockSpec(memory_space=pltpu.VMEM),
        scratch_shapes=[
            pltpu.VMEM((chunks, PARTS) + piece, dtype),
            pltpu.VMEM((bins // run, 2 * LANES, 2 * LANES), dtype),
            pltpu.VMEM((PAIRED, slices, 2, bins // slices, sources // 2 * LANES), dtype),
            pltpu.VMEM((steps, sources, receivers, lags), jnp.float32),
            pltpu.VMEM((steps, members - 1) + kept, dtype),
            pltpu.VMEM((chunks, PARTS) + piece, dtype),
            pltpu.VMEM((steps, sources, receivers, lags), dtype),
            pltpu.VMEM((chunks, 2) + piece, dtype),
            pltpu.VMEM((chunks, 2) + piece, dtype),
        ]
        + [pltpu.VMEM((chunks,) + piece, dtype)] * 6
        + [pltpu.SemaphoreType.DMA((chunks,))] * 10
        + [pltpu.SemaphoreType.DMA((chunks, 2))] * 2
        + [pltpu.SemaphoreType.DMA((steps, members - 1))] * 2,
        compiler_params=pltpu.CompilerParams(
            collective_id=0, has_side_effects=True, vmem_limit_bytes=60 << 20
        ),
    )(owners, blocks, spectra, table, places, max_lag)


def body(spectra, owners, blocks, max_lag):
    window_count, _, _, bin_count = spectra.shape
    group_count = lax.axis_size("win")
    run = LANES // (2 * window_count)
    slices = bin_count // (PARTS * LANES)
    table = jnp.asarray(lag_rows(bin_count, LAGS, window_count * group_count, slices))
    places = jnp.asarray(placement(spectra.shape[1]))
    return main(spectra, table, places, owners, blocks, max_lag, run)


def solution(mesh):
    return jax.shard_map(
        body,
        mesh=mesh,
        in_specs=(P("win", "chan", None, None), P(), P(), P(None, "win", "chan")),
        out_specs=P(None, "win", "chan", None),
        check_vma=False,
    )
```

```python
import functools

import jax
import jax.numpy as jnp
import numpy as np
from jax import lax
from jax.experimental import pallas as pl
from jax.experimental.pallas import tpu as pltpu
from jax.sharding import PartitionSpec as P

SRC = 16
STEPS = 4
LAGS = 128
LANES = 128
PARTS = 4
PAIRED = 2
KIB = 56 << 10


def lag_rows(bin_count, lag_count, window_count, slices):
    bins = np.arange(bin_count, dtype=np.int64)[None, :]
    offsets = np.arange(lag_count, dtype=np.int64)[:, None] - lag_count // 2
    phase = (bins * offsets % (2 * bin_count)) * (np.pi / bin_count)
    weight = np.where(bins == 0, 1.0, 2.0) / np.sqrt(2.0 * bin_count * window_count)
    rows = np.stack([weight * np.cos(phase), -weight * np.sin(phase)], 1)
    rows = rows.reshape(lag_count, 2, slices, bin_count // slices).transpose(2, 0, 1, 3)
    return rows.reshape(slices, lag_count, -1).astype(np.float32).astype(jnp.bfloat16)


def placement(receivers):
    places = np.zeros((2, 2, 2 * receivers, 4, receivers), np.float32)
    c = np.arange(receivers)
    for half in range(2):
        places[half, 0, 2 * c, half, c] = 1
        places[half, 0, 2 * c + 1, 2 + half, c] = -1
        places[half, 1, 2 * c + 1, half, c] = 1
        places[half, 1, 2 * c, 2 + half, c] = 1
    return places.reshape(4, 2 * receivers, 4 * receivers).astype(jnp.bfloat16)


def main_kernel(
    owners_ref, blocks_ref, spectra_in, lag_in, place_in, limit_ref, out_ref,
    spectra_ref, lag_ref, place_ref, loaded,
    own, weights, cross_spectra, made, arrived, got,
    sent, from_core, half, from_cross, quarter, from_low, from_high, to_high, to_low,
    core_send, core_recv, cross_send, cross_recv, up_send, up_recv,
    down_send, down_recv, share_send, share_recv, last_send, last_recv,
    sum_send, sum_recv,
    *, length, members, run,
):
    chunks, parts, paired, groups, sources, width = own.shape
    slices = lag_ref.shape[0]
    steps = chunks // slices * paired
    pairs = sources // 2
    windows, receivers, _, bins = spectra_ref.shape
    terms = 2 * windows
    kept = sources // members
    me = lax.axis_index("chan")
    win = lax.axis_index("win")
    line, cross, core = me // 4, (me // 2) % 2, me % 2
    core_peer = me + 1 - 2 * core
    cross_peer = me + 2 - 4 * cross
    mine = 2 * core + cross
    theirs = 2 * core + 1 - cross
    has_low, has_high = line > 0, line < length - 1
    near_low = line < length // 2

    def remote(src, dst, send, recv, peer):
        return pltpu.make_async_remote_copy(
            src_ref=src, dst_ref=dst, send_sem=send, recv_sem=recv,
            device_id={"chan": peer}, device_id_type=pl.DeviceIdType.MESH,
        )

    def to_core(s):
        part = own.at[s, pl.ds(2 * (1 - core), 2)]
        return remote(part, from_core.at[s], core_send.at[s], core_recv.at[s], core_peer)

    def to_cross(s):
        return remote(
            half.at[s, 1 - cross], from_cross.at[s], cross_send.at[s], cross_recv.at[s],
            cross_peer,
        )

    def go_up(s):
        return remote(to_high.at[s], from_low.at[s], up_send.at[s], up_recv.at[s], me + 4)

    def go_down(s):
        return remote(to_low.at[s], from_high.at[s], down_send.at[s], down_recv.at[s], me - 4)

    def share(s):
        ref = got.at[s, mine]
        return remote(ref, ref, share_send.at[s], share_recv.at[s], cross_peer)

    def last(s, which, index):
        ref = got.at[s, index]
        return remote(ref, ref, last_send.at[s, which], last_recv.at[s, which], core_peer)

    def add_up(s, j):
        peer = (win + j) % members
        return pltpu.make_async_remote_copy(
            src_ref=sent.at[s, pl.ds(peer * kept, kept)],
            dst_ref=arrived.at[s, j - 1],
            send_sem=sum_send.at[s, j - 1],
            recv_sem=sum_recv.at[s, j - 1],
            device_id={"win": peer},
            device_id_type=pl.DeviceIdType.MESH,
        )

    loads = [
        pltpu.make_async_copy(src, dst, loaded.at[k])
        for k, (src, dst) in enumerate(
            ((spectra_in, spectra_ref), (place_in, place_ref), (lag_in, lag_ref))
        )
    ]
    for load in loads:
        load.start()

    barrier = pltpu.get_barrier_semaphore()

    def greet(peer):
        pl.semaphore_signal(
            barrier, inc=1, device_id={"chan": peer}, device_id_type=pl.DeviceIdType.MESH
        )

    greet(core_peer)
    greet(cross_peer)
    for j in range(1, members):
        pl.semaphore_signal(
            barrier,
            inc=1,
            device_id={"win": (win + j) % members},
            device_id_type=pl.DeviceIdType.MESH,
        )

    @pl.when(has_low)
    def _():
        greet(me - 4)

    @pl.when(has_high)
    def _():
        greet(me + 4)

    pl.semaphore_wait(
        barrier, 1 + members + jnp.where(has_low, 1, 0) + jnp.where(has_high, 1, 0)
    )

    def single(s):
        return s >= chunks - paired

    def step_of(s, i):
        return jnp.where(single(s), s - chunks + steps, s // slices * paired + i)

    def slice_of(s, i):
        return jnp.where(single(s), slices - paired + i, s % slices)

    def choose(ref, s, mine_if, own, other):
        for i in range(paired):
            ref[s, i] = lax.select(mine_if(owners_ref[step_of(s, i)]), own[i], other[i])

    block = lax.broadcasted_iota(jnp.int32, (sources, LANES), 1) // run
    odd = [(block // bit) % 2 == 1 for bit in (1, 2, 4)]

    def choice(step):
        shape = (2 * sources, 2 * receivers)
        row = lax.broadcasted_iota(jnp.int32, shape, 0)
        column = lax.broadcasted_iota(jnp.int32, shape, 1)
        wanted = 2 * (blocks_ref[step] * sources + row % sources) + row // sources
        return jnp.where(column == wanted, 1.0, 0.0).astype(jnp.bfloat16)

    def channels(w, at, size):
        return spectra_ref[w, :, :, at].reshape(2 * receivers, size)

    def lay(s):
        for two in range(parts // 2):
            for j in range(paired):
                picks = choice(step_of(s, j))
                q = slice_of(s, j) * parts + 2 * two
                at = pl.ds(pl.multiple_of(q * LANES, 2 * LANES), 2 * LANES)
                found = [
                    jnp.dot(picks, channels(w, at, 2 * LANES), preferred_element_type=jnp.float32)
                    for w in range(windows)
                ]
                for e in range(2):
                    tiles = []
                    for i in range(terms):
                        top = i % 2 * sources
                        tile = found[i // 2][top : top + sources, e * LANES : (e + 1) * LANES]
                        tiles.append(pltpu.roll(tile, i * run, 1) if i else tile)
                    for k, mask in enumerate(odd):
                        tiles = [
                            jnp.where(mask, tiles[(i + (1 << k)) % terms], tiles[i])
                            for i in range(terms)
                        ]
                    wide = [
                        jnp.concatenate([tiles[-g % terms][:pairs], tiles[-g % terms][pairs:]], 1)
                        for g in range(2 * groups)
                    ]
                    for g in range(groups):
                        own[s, 2 * two + e, j, g] = jnp.concatenate(
                            wide[2 * g : 2 * g + 2], 0
                        ).astype(jnp.bfloat16)

    def leave(s):
        to_core(s).wait_recv()
        for i in range(paired):
            owner = owners_ref[step_of(s, i)]
            for k in range(2):
                half[s, k, i] = lax.select(
                    owner == me, own[s, 2 * core + k, i], from_core[s, k, i]
                )
        to_cross(s).start()

    loads[0].wait()

    @pl.loop(0, chunks + 1)
    def _(t):
        @pl.when(t < chunks)
        def _():
            lay(t)
            to_core(t).start()

        @pl.when(t >= 1)
        def _():
            leave(t - 1)

    def weigh(b):
        @pl.loop(0, PARTS)
        def _(part):
            q = b * PARTS + part
            at = pl.ds(pl.multiple_of(q * LANES, LANES), LANES)
            for w in range(windows):
                turned = channels(w, at, LANES).T
                for k in range(4):
                    tile = jnp.dot(
                        turned, place_ref[k], preferred_element_type=jnp.float32
                    ).astype(jnp.bfloat16)
                    for g in range(2 * groups):
                        row = (k // 2) * LANES + (2 * w + k % 2 + g) % terms * run
                        weights[q * 2 * groups + g, row : row + run] = tile[
                            g * run : (g + 1) * run
                        ]

    def limits():
        same = lax.broadcasted_iota(jnp.int32, (receivers, receivers), 0) == (
            lax.broadcasted_iota(jnp.int32, (receivers, receivers), 1)
        )
        for s in range(steps):
            for k in range(kept):
                line_of = limit_ref[s, k : k + 1].astype(jnp.float32)
                column = jnp.where(same, jnp.broadcast_to(line_of, same.shape), 0.0)
                column = jnp.sum(column, axis=1, keepdims=True)
                out_ref[s, k] = jnp.broadcast_to(column, out_ref.shape[2:])

    lane = lax.broadcasted_iota(jnp.int32, (run, width), 1) % run
    row = lax.broadcasted_iota(jnp.int32, (run, width), 0)
    keep = (lane == row).astype(jnp.float32)

    def spread(value, e):
        return [
            (jnp.broadcast_to(value[r : r + 1], (run, width)) * keep).astype(jnp.bfloat16)
            for r in range(e * pairs, (e + 1) * pairs)
        ]

    def multiply(rows, which):
        dots = jnp.dot(
            jnp.concatenate(rows, 0), weights[which], preferred_element_type=jnp.float32
        )
        return dots.astype(jnp.bfloat16)

    def keep_products(s, i, part, at, dots):
        base = pl.multiple_of((part * 2 * groups + at) * run, run)
        buffer, piece = step_of(s, i) % paired, slice_of(s, i)
        for p in range(pairs):
            one = dots[p * run : (p + 1) * run]
            to = slice(p * LANES, (p + 1) * LANES)
            cross_spectra[buffer, piece, 0, pl.ds(base, run), to] = one[:, :LANES]
            cross_spectra[buffer, piece, 1, pl.ds(base, run), to] = one[:, LANES:]

    def cross_part(s, part):
        first = (s % slices * parts + part) * 2 * groups
        for g in range(groups):
            values = [got[s, part, i, g].astype(jnp.float32) for i in range(paired)]
            for e in range(2):
                at = 2 * g + e
                dots = multiply(spread(values[0], e) + spread(values[1], e), first + at)
                for i in range(paired):
                    keep_products(s, i, part, at, dots[i * pairs * run : (i + 1) * pairs * run])

    def cross_single(s, part):
        for i in range(paired):
            first = (slice_of(s, i) * parts + part) * 2 * groups
            for g in range(groups):
                value = got[s, part, i, g].astype(jnp.float32)
                for e in range(2):
                    at = 2 * g + e
                    keep_products(s, i, part, at, multiply(spread(value, e), first + at))

    def lag_part(step, b, last_one):
        for n in range(pairs // 2):
            at = slice(n * 2 * LANES, (n + 1) * 2 * LANES)
            values = jnp.concatenate(
                [cross_spectra[step % paired, b + k // 2, k % 2, :, at] for k in range(4)], 0
            )
            table = jnp.concatenate([lag_ref[b], lag_ref[b + 1]], 1)
            turned = jnp.dot(table, values, preferred_element_type=jnp.float32).T
            for k in range(4):
                source = 2 * n + k // 2 + (k % 2) * pairs
                one = turned[k * receivers : (k + 1) * receivers]
                if not last_one:
                    made[step, source] = one
                    continue
                one += made[step, source]
                made[step, source] = one
                sent[step, source] = one.astype(jnp.bfloat16)
        if last_one:
            for j in range(1, members):
                add_up(step, j).start()

    def low_side(s):
        @pl.when(has_low)
        def _():
            go_up(s).wait_recv()
            choose(to_high, s, lambda o: o // 4 == line, quarter[s], from_low[s])

            @pl.when(has_high)
            def _():
                go_up(s).start()

    def high_side(s):
        @pl.when(has_high)
        def _():
            go_down(s).wait_recv()
            choose(to_low, s, lambda o: o // 4 == line, quarter[s], from_high[s])

            @pl.when(has_low)
            def _():
                go_down(s).start()

    def enter(s):
        to_cross(s).wait_recv()

        choose(quarter, s, lambda o: (o // 2) % 2 == cross, half[s, cross], from_cross[s])

        @pl.when(line == 0)
        def _():
            to_high[s] = quarter[s]
            go_up(s).start()

        @pl.when(line == length - 1)
        def _():
            to_low[s] = quarter[s]
            go_down(s).start()

    def near_side(s):
        @pl.when(near_low)
        def _():
            low_side(s)

        @pl.when(jnp.logical_not(near_low))
        def _():
            high_side(s)

    def far_side(s):
        @pl.when(near_low)
        def _():
            high_side(s)

        @pl.when(jnp.logical_not(near_low))
        def _():
            low_side(s)

    inner = (line > 0) & (line < length - 1)

    def settle(s):
        @pl.when(jnp.logical_not(inner))
        def _():
            far_side(s)

        choose(got.at[:, mine], s, lambda o: o // 4 <= line, to_high[s], to_low[s])
        share(s).start()
        last(s, 0, mine).start()

    def pass_on(s):
        share(s).wait_recv()
        last(s, 1, theirs).start()

    limits()
    loads[1].wait()
    loads[2].wait()

    def at(t, delay):
        return (t >= delay) & (t < chunks + delay)

    @pl.loop(0, chunks + 8)
    def _(t):
        @pl.when(t < chunks)
        def _():
            enter(t)

        @pl.when(at(t, 2))
        def _():
            near_side(t - 2)

        @pl.when(at(t, 4) & inner)
        def _():
            far_side(t - 4)

        @pl.when(at(t, 6))
        def _():
            settle(t - 6)

        @pl.when(t >= 8)
        def _():
            pass_on(t - 8)

        @pl.when(t < slices)
        def _():
            weigh(t)

        def finish(s, cross_of):
            cross_of(s, mine)
            cross_of(s, theirs)
            for which in range(2):
                last(s, which, mine).wait_recv()
            cross_of(s, 2 * (1 - core))
            cross_of(s, 2 * (1 - core) + 1)

        @pl.when((t >= 8) & (t - 8 < chunks - paired))
        def _():
            s = t - 8
            finish(s, cross_part)

            @pl.when(s % slices == slices // 2 - 1)
            def _():
                for i in range(paired):
                    lag_part(s // slices * paired + i, 0, False)

            @pl.when(s % slices == slices - 1)
            def _():
                for i in range(paired):
                    lag_part(s // slices * paired + i, slices - 2, True)

        @pl.when(t - 8 >= chunks - paired)
        def _():
            s = t - 8
            finish(s, cross_single)
            lag_part(step_of(s, 0), slices - 2, True)

    @pl.loop(0, chunks)
    def _(s):
        to_core(s).wait_send()
        to_cross(s).wait_send()
        share(s).wait_send()
        for which in range(2):
            last(s, which, mine).wait_send()

        @pl.when(has_high)
        def _():
            go_up(s).wait_send()

        @pl.when(has_low)
        def _():
            go_down(s).wait_send()

    @pl.loop(0, steps)
    def _(s):
        total = made[s, pl.ds(win * kept, kept)]
        for j in range(1, members):
            add_up(s, j).wait()
            total += arrived[s, j - 1].astype(jnp.float32)
        offset = lax.broadcasted_iota(jnp.int32, total.shape, 2) - total.shape[2] // 2
        inside = jnp.abs(offset).astype(jnp.float32) <= out_ref[s]
        out_ref[s] = jnp.where(inside, total, 0.0)


def main(spectra, table, places, owners, blocks, max_lag, run):
    windows, receivers, _, bins = spectra.shape
    members = lax.axis_size("win")
    slices, lags, _ = table.shape
    steps, sources, dtype = STEPS, SRC, spectra.dtype
    chunks = steps // PAIRED * slices
    piece = (PAIRED, LANES // run // 2, sources, 2 * LANES)
    kept = (sources // members, receivers, lags)
    return pl.pallas_call(
        functools.partial(
            main_kernel, length=lax.axis_size("chan") // 4, members=members, run=run
        ),
        out_shape=jax.ShapeDtypeStruct((steps,) + kept, jnp.float32),
        in_specs=[pl.BlockSpec(memory_space=pltpu.SMEM)] * 2
        + [pl.BlockSpec(memory_space=pltpu.HBM)] * 3
        + [pl.BlockSpec(memory_space=pltpu.VMEM)],
        out_specs=pl.BlockSpec(memory_space=pltpu.VMEM),
        scratch_shapes=[
            pltpu.VMEM(spectra.shape, dtype),
            pltpu.VMEM(table.shape, dtype),
            pltpu.VMEM(places.shape, dtype),
            pltpu.SemaphoreType.DMA((3,)),
            pltpu.VMEM((chunks, PARTS) + piece, dtype),
            pltpu.VMEM((bins // run, 2 * LANES, 2 * LANES), dtype),
            pltpu.VMEM((PAIRED, slices, 2, bins // slices, sources // 2 * LANES), dtype),
            pltpu.VMEM((steps, sources, receivers, lags), jnp.float32),
            pltpu.VMEM((steps, members - 1) + kept, dtype),
            pltpu.VMEM((chunks, PARTS) + piece, dtype),
            pltpu.VMEM((steps, sources, receivers, lags), dtype),
            pltpu.VMEM((chunks, 2) + piece, dtype),
            pltpu.VMEM((chunks, 2) + piece, dtype),
        ]
        + [pltpu.VMEM((chunks,) + piece, dtype)] * 6
        + [pltpu.SemaphoreType.DMA((chunks,))] * 10
        + [pltpu.SemaphoreType.DMA((chunks, 2))] * 2
        + [pltpu.SemaphoreType.DMA((steps, members - 1))] * 2,
        compiler_params=pltpu.CompilerParams(
            collective_id=0, has_side_effects=True, vmem_limit_bytes=KIB << 10
        ),
    )(owners, blocks, spectra, table, places, max_lag)


def body(spectra, owners, blocks, max_lag):
    window_count, _, _, bin_count = spectra.shape
    group_count = lax.axis_size("win")
    run = LANES // (2 * window_count)
    slices = bin_count // (PARTS * LANES)
    table = jnp.asarray(lag_rows(bin_count, LAGS, window_count * group_count, slices))
    places = jnp.asarray(placement(spectra.shape[1]))
    return main(spectra, table, places, owners, blocks, max_lag, run)


def solution(mesh):
    return jax.shard_map(
        body,
        mesh=mesh,
        in_specs=(P("win", "chan", None, None), P(), P(), P(None, "win", "chan")),
        out_specs=P(None, "win", "chan", None),
        check_vma=False,
    )
```

```python
import functools

import jax
import jax.numpy as jnp
import numpy as np
from jax import lax
from jax.experimental import pallas as pl
from jax.experimental.pallas import tpu as pltpu
from jax.sharding import PartitionSpec as P

SRC = 16
STEPS = 4
LAGS = 128
LANES = 128
PARTS = 4
PAIRED = 2
KIB = 56 << 10


def lag_rows(bin_count, lag_count, window_count, slices):
    bins = np.arange(bin_count, dtype=np.int64)[None, :]
    offsets = np.arange(lag_count, dtype=np.int64)[:, None] - lag_count // 2
    phase = (bins * offsets % (2 * bin_count)) * (np.pi / bin_count)
    weight = np.where(bins == 0, 1.0, 2.0) / np.sqrt(2.0 * bin_count * window_count)
    rows = np.stack([weight * np.cos(phase), -weight * np.sin(phase)], 1)
    rows = rows.reshape(lag_count, 2, slices, bin_count // slices).transpose(2, 0, 1, 3)
    return rows.reshape(slices, lag_count, -1).astype(np.float32).astype(jnp.bfloat16)


def placement(receivers):
    places = np.zeros((2, 2, 2 * receivers, 4, receivers), np.float32)
    c = np.arange(receivers)
    for half in range(2):
        places[half, 0, 2 * c, half, c] = 1
        places[half, 0, 2 * c + 1, 2 + half, c] = -1
        places[half, 1, 2 * c + 1, half, c] = 1
        places[half, 1, 2 * c, 2 + half, c] = 1
    return places.reshape(4, 2 * receivers, 4 * receivers).astype(jnp.bfloat16)


def main_kernel(
    owners_ref, blocks_ref, spectra_in, lag_in, place_in, limit_ref, out_ref,
    spectra_ref, lag_ref, place_ref, loaded,
    own, weights, cross_spectra, made, arrived, got,
    sent, from_core, half, from_cross, quarter, from_low, from_high, to_high, to_low,
    core_send, core_recv, cross_send, cross_recv, up_send, up_recv,
    down_send, down_recv, share_send, share_recv, last_send, last_recv,
    sum_send, sum_recv,
    *, length, members, run,
):
    chunks, parts, paired, groups, sources, width = own.shape
    slices = lag_ref.shape[0]
    steps = chunks // slices * paired
    pairs = sources // 2
    windows, receivers, _, bins = spectra_ref.shape
    terms = 2 * windows
    kept = sources // members
    me = lax.axis_index("chan")
    win = lax.axis_index("win")
    line, cross, core = me // 4, (me // 2) % 2, me % 2
    core_peer = me + 1 - 2 * core
    cross_peer = me + 2 - 4 * cross
    mine = 2 * core + cross
    theirs = 2 * core + 1 - cross
    has_low, has_high = line > 0, line < length - 1
    near_low = line < length // 2

    def remote(src, dst, send, recv, peer):
        return pltpu.make_async_remote_copy(
            src_ref=src, dst_ref=dst, send_sem=send, recv_sem=recv,
            device_id={"chan": peer}, device_id_type=pl.DeviceIdType.MESH,
        )

    def to_core(s):
        part = own.at[s, pl.ds(2 * (1 - core), 2)]
        return remote(part, from_core.at[s], core_send.at[s], core_recv.at[s], core_peer)

    def to_cross(s):
        return remote(
            half.at[s, 1 - cross], from_cross.at[s], cross_send.at[s], cross_recv.at[s],
            cross_peer,
        )

    def go_up(s):
        return remote(to_high.at[s], from_low.at[s], up_send.at[s], up_recv.at[s], me + 4)

    def go_down(s):
        return remote(to_low.at[s], from_high.at[s], down_send.at[s], down_recv.at[s], me - 4)

    def share(s):
        ref = got.at[s, mine]
        return remote(ref, ref, share_send.at[s], share_recv.at[s], cross_peer)

    def last(s, which, index):
        ref = got.at[s, index]
        return remote(ref, ref, last_send.at[s, which], last_recv.at[s, which], core_peer)

    def add_up(s, j):
        peer = (win + j) % members
        return pltpu.make_async_remote_copy(
            src_ref=sent.at[s, pl.ds(peer * kept, kept)],
            dst_ref=arrived.at[s, j - 1],
            send_sem=sum_send.at[s, j - 1],
            recv_sem=sum_recv.at[s, j - 1],
            device_id={"win": peer},
            device_id_type=pl.DeviceIdType.MESH,
        )

    loads = [
        pltpu.make_async_copy(src, dst, loaded.at[k])
        for k, (src, dst) in enumerate(
            ((spectra_in, spectra_ref), (place_in, place_ref), (lag_in, lag_ref))
        )
    ]
    for load in loads:
        load.start()

    barrier = pltpu.get_barrier_semaphore()

    def greet(peer):
        pl.semaphore_signal(
            barrier, inc=1, device_id={"chan": peer}, device_id_type=pl.DeviceIdType.MESH
        )

    greet(core_peer)
    greet(cross_peer)
    for j in range(1, members):
        pl.semaphore_signal(
            barrier,
            inc=1,
            device_id={"win": (win + j) % members},
            device_id_type=pl.DeviceIdType.MESH,
        )

    @pl.when(has_low)
    def _():
        greet(me - 4)

    @pl.when(has_high)
    def _():
        greet(me + 4)

    pl.semaphore_wait(
        barrier, 1 + members + jnp.where(has_low, 1, 0) + jnp.where(has_high, 1, 0)
    )

    def single(s):
        return s >= chunks - paired

    def step_of(s, i):
        return jnp.where(single(s), s - chunks + steps, s // slices * paired + i)

    def slice_of(s, i):
        return jnp.where(single(s), slices - paired + i, s % slices)

    def choose(ref, s, mine_if, own, other):
        for i in range(paired):
            ref[s, i] = lax.select(mine_if(owners_ref[step_of(s, i)]), own[i], other[i])

    block = lax.broadcasted_iota(jnp.int32, (sources, LANES), 1) // run
    odd = [(block // bit) % 2 == 1 for bit in (1, 2, 4)]

    def choice(step):
        shape = (2 * sources, 2 * receivers)
        row = lax.broadcasted_iota(jnp.int32, shape, 0)
        column = lax.broadcasted_iota(jnp.int32, shape, 1)
        wanted = 2 * (blocks_ref[step] * sources + row % sources) + row // sources
        return jnp.where(column == wanted, 1.0, 0.0).astype(jnp.bfloat16)

    def channels(w, at, size):
        return spectra_ref[w, :, :, at].reshape(2 * receivers, size)

    def lay(s):
        for two in range(parts // 2):
            for j in range(paired):
                picks = choice(step_of(s, j))
                q = slice_of(s, j) * parts + 2 * two
                at = pl.ds(pl.multiple_of(q * LANES, 2 * LANES), 2 * LANES)
                found = [
                    jnp.dot(picks, channels(w, at, 2 * LANES), preferred_element_type=jnp.float32)
                    for w in range(windows)
                ]
                for e in range(2):
                    tiles = []
                    for i in range(terms):
                        top = i % 2 * sources
                        tile = found[i // 2][top : top + sources, e * LANES : (e + 1) * LANES]
                        tiles.append(pltpu.roll(tile, i * run, 1) if i else tile)
                    for k, mask in enumerate(odd):
                        tiles = [
                            jnp.where(mask, tiles[(i + (1 << k)) % terms], tiles[i])
                            for i in range(terms)
                        ]
                    wide = [
                        jnp.concatenate([tiles[-g % terms][:pairs], tiles[-g % terms][pairs:]], 1)
                        for g in range(2 * groups)
                    ]
                    for g in range(groups):
                        own[s, 2 * two + e, j, g] = jnp.concatenate(
                            wide[2 * g : 2 * g + 2], 0
                        ).astype(jnp.bfloat16)

    def leave(s):
        to_core(s).wait_recv()
        for i in range(paired):
            owner = owners_ref[step_of(s, i)]
            for k in range(2):
                half[s, k, i] = lax.select(
                    owner == me, own[s, 2 * core + k, i], from_core[s, k, i]
                )
        to_cross(s).start()

    loads[0].wait()

    @pl.loop(0, chunks + 1)
    def _(t):
        @pl.when(t < chunks)
        def _():
            lay(t)
            to_core(t).start()

        @pl.when(t >= 1)
        def _():
            leave(t - 1)

    def weigh(b):
        @pl.loop(0, PARTS)
        def _(part):
            q = b * PARTS + part
            at = pl.ds(pl.multiple_of(q * LANES, LANES), LANES)
            for w in range(windows):
                turned = channels(w, at, LANES).T
                for k in range(4):
                    tile = jnp.dot(
                        turned, place_ref[k], preferred_element_type=jnp.float32
                    ).astype(jnp.bfloat16)
                    for g in range(2 * groups):
                        row = (k // 2) * LANES + (2 * w + k % 2 + g) % terms * run
                        weights[q * 2 * groups + g, row : row + run] = tile[
                            g * run : (g + 1) * run
                        ]

    def limits():
        same = lax.broadcasted_iota(jnp.int32, (receivers, receivers), 0) == (
            lax.broadcasted_iota(jnp.int32, (receivers, receivers), 1)
        )
        for s in range(steps):
            for k in range(kept):
                line_of = limit_ref[s, k : k + 1].astype(jnp.float32)
                column = jnp.where(same, jnp.broadcast_to(line_of, same.shape), 0.0)
                column = jnp.sum(column, axis=1, keepdims=True)
                out_ref[s, k] = jnp.broadcast_to(column, out_ref.shape[2:])

    lane = lax.broadcasted_iota(jnp.int32, (run, width), 1) % run
    row = lax.broadcasted_iota(jnp.int32, (run, width), 0)
    keep = (lane == row).astype(jnp.float32)

    def spread(value, e):
        return [
            (jnp.broadcast_to(value[r : r + 1], (run, width)) * keep).astype(jnp.bfloat16)
            for r in range(e * pairs, (e + 1) * pairs)
        ]

    def multiply(rows, which):
        dots = jnp.dot(
            jnp.concatenate(rows, 0), weights[which], preferred_element_type=jnp.float32
        )
        return dots.astype(jnp.bfloat16)

    def keep_products(s, i, part, at, dots):
        base = pl.multiple_of((part * 2 * groups + at) * run, run)
        buffer, piece = step_of(s, i) % paired, slice_of(s, i)
        for p in range(pairs):
            one = dots[p * run : (p + 1) * run]
            to = slice(p * LANES, (p + 1) * LANES)
            cross_spectra[buffer, piece, 0, pl.ds(base, run), to] = one[:, :LANES]
            cross_spectra[buffer, piece, 1, pl.ds(base, run), to] = one[:, LANES:]

    def cross_part(s, part):
        first = (s % slices * parts + part) * 2 * groups
        for g in range(groups):
            values = [got[s, part, i, g].astype(jnp.float32) for i in range(paired)]
            for e in range(2):
                at = 2 * g + e
                dots = multiply(spread(values[0], e) + spread(values[1], e), first + at)
                for i in range(paired):
                    keep_products(s, i, part, at, dots[i * pairs * run : (i + 1) * pairs * run])

    def cross_single(s, part):
        for i in range(paired):
            first = (slice_of(s, i) * parts + part) * 2 * groups
            for g in range(groups):
                value = got[s, part, i, g].astype(jnp.float32)
                for e in range(2):
                    at = 2 * g + e
                    keep_products(s, i, part, at, multiply(spread(value, e), first + at))

    def lag_part(step, b, last_one):
        for n in range(pairs // 2):
            at = slice(n * 2 * LANES, (n + 1) * 2 * LANES)
            values = jnp.concatenate(
                [cross_spectra[step % paired, b + k // 2, k % 2, :, at] for k in range(4)], 0
            )
            table = jnp.concatenate([lag_ref[b], lag_ref[b + 1]], 1)
            turned = jnp.dot(table, values, preferred_element_type=jnp.float32).T
            for k in range(4):
                source = 2 * n + k // 2 + (k % 2) * pairs
                one = turned[k * receivers : (k + 1) * receivers]
                if not last_one:
                    made[step, source] = one
                    continue
                one += made[step, source]
                made[step, source] = one
                sent[step, source] = one.astype(jnp.bfloat16)
        if last_one:
            for j in range(1, members):
                add_up(step, j).start()

    def low_side(s):
        @pl.when(has_low)
        def _():
            go_up(s).wait_recv()
            choose(to_high, s, lambda o: o // 4 == line, quarter[s], from_low[s])

            @pl.when(has_high)
            def _():
                go_up(s).start()

    def high_side(s):
        @pl.when(has_high)
        def _():
            go_down(s).wait_recv()
            choose(to_low, s, lambda o: o // 4 == line, quarter[s], from_high[s])

            @pl.when(has_low)
            def _():
                go_down(s).start()

    def enter(s):
        to_cross(s).wait_recv()

        choose(quarter, s, lambda o: (o // 2) % 2 == cross, half[s, cross], from_cross[s])

        @pl.when(line == 0)
        def _():
            to_high[s] = quarter[s]
            go_up(s).start()

        @pl.when(line == length - 1)
        def _():
            to_low[s] = quarter[s]
            go_down(s).start()

    def near_side(s):
        @pl.when(near_low)
        def _():
            low_side(s)

        @pl.when(jnp.logical_not(near_low))
        def _():
            high_side(s)

    def far_side(s):
        @pl.when(near_low)
        def _():
            high_side(s)

        @pl.when(jnp.logical_not(near_low))
        def _():
            low_side(s)

    inner = (line > 0) & (line < length - 1)

    def settle(s):
        @pl.when(jnp.logical_not(inner))
        def _():
            far_side(s)

        choose(got.at[:, mine], s, lambda o: o // 4 <= line, to_high[s], to_low[s])
        share(s).start()
        last(s, 0, mine).start()

    def pass_on(s):
        share(s).wait_recv()
        last(s, 1, theirs).start()

    limits()
    loads[1].wait()
    loads[2].wait()

    def at(t, delay):
        return (t >= delay) & (t < chunks + delay)

    @pl.loop(0, chunks + 8)
    def _(t):
        @pl.when(t >= 8)
        def _():
            pass_on(t - 8)

        @pl.when(at(t, 6))
        def _():
            settle(t - 6)

        @pl.when(at(t, 4) & inner)
        def _():
            far_side(t - 4)

        @pl.when(at(t, 2))
        def _():
            near_side(t - 2)

        @pl.when(t < chunks)
        def _():
            enter(t)

        @pl.when(t < slices)
        def _():
            weigh(t)

        def finish(s, cross_of):
            cross_of(s, mine)
            cross_of(s, theirs)
            for which in range(2):
                last(s, which, mine).wait_recv()
            cross_of(s, 2 * (1 - core))
            cross_of(s, 2 * (1 - core) + 1)

        @pl.when((t >= 8) & (t - 8 < chunks - paired))
        def _():
            s = t - 8
            finish(s, cross_part)

            @pl.when(s % slices == slices // 2 - 1)
            def _():
                for i in range(paired):
                    lag_part(s // slices * paired + i, 0, False)

            @pl.when(s % slices == slices - 1)
            def _():
                for i in range(paired):
                    lag_part(s // slices * paired + i, slices - 2, True)

        @pl.when(t - 8 >= chunks - paired)
        def _():
            s = t - 8
            finish(s, cross_single)
            lag_part(step_of(s, 0), slices - 2, True)

    @pl.loop(0, chunks)
    def _(s):
        to_core(s).wait_send()
        to_cross(s).wait_send()
        share(s).wait_send()
        for which in range(2):
            last(s, which, mine).wait_send()

        @pl.when(has_high)
        def _():
            go_up(s).wait_send()

        @pl.when(has_low)
        def _():
            go_down(s).wait_send()

    @pl.loop(0, steps)
    def _(s):
        total = made[s, pl.ds(win * kept, kept)]
        for j in range(1, members):
            add_up(s, j).wait()
            total += arrived[s, j - 1].astype(jnp.float32)
        offset = lax.broadcasted_iota(jnp.int32, total.shape, 2) - total.shape[2] // 2
        inside = jnp.abs(offset).astype(jnp.float32) <= out_ref[s]
        out_ref[s] = jnp.where(inside, total, 0.0)


def main(spectra, table, places, owners, blocks, max_lag, run):
    windows, receivers, _, bins = spectra.shape
    members = lax.axis_size("win")
    slices, lags, _ = table.shape
    steps, sources, dtype = STEPS, SRC, spectra.dtype
    chunks = steps // PAIRED * slices
    piece = (PAIRED, LANES // run // 2, sources, 2 * LANES)
    kept = (sources // members, receivers, lags)
    return pl.pallas_call(
        functools.partial(
            main_kernel, length=lax.axis_size("chan") // 4, members=members, run=run
        ),
        out_shape=jax.ShapeDtypeStruct((steps,) + kept, jnp.float32),
        in_specs=[pl.BlockSpec(memory_space=pltpu.SMEM)] * 2
        + [pl.BlockSpec(memory_space=pltpu.HBM)] * 3
        + [pl.BlockSpec(memory_space=pltpu.VMEM)],
        out_specs=pl.BlockSpec(memory_space=pltpu.VMEM),
        scratch_shapes=[
            pltpu.VMEM(spectra.shape, dtype),
            pltpu.VMEM(table.shape, dtype),
            pltpu.VMEM(places.shape, dtype),
            pltpu.SemaphoreType.DMA((3,)),
            pltpu.VMEM((chunks, PARTS) + piece, dtype),
            pltpu.VMEM((bins // run, 2 * LANES, 2 * LANES), dtype),
            pltpu.VMEM((PAIRED, slices, 2, bins // slices, sources // 2 * LANES), dtype),
            pltpu.VMEM((steps, sources, receivers, lags), jnp.float32),
            pltpu.VMEM((steps, members - 1) + kept, dtype),
            pltpu.VMEM((chunks, PARTS) + piece, dtype),
            pltpu.VMEM((steps, sources, receivers, lags), dtype),
            pltpu.VMEM((chunks, 2) + piece, dtype),
            pltpu.VMEM((chunks, 2) + piece, dtype),
        ]
        + [pltpu.VMEM((chunks,) + piece, dtype)] * 6
        + [pltpu.SemaphoreType.DMA((chunks,))] * 10
        + [pltpu.SemaphoreType.DMA((chunks, 2))] * 2
        + [pltpu.SemaphoreType.DMA((steps, members - 1))] * 2,
        compiler_params=pltpu.CompilerParams(
            collective_id=0, has_side_effects=True, vmem_limit_bytes=KIB << 10
        ),
    )(owners, blocks, spectra, table, places, max_lag)


def body(spectra, owners, blocks, max_lag):
    window_count, _, _, bin_count = spectra.shape
    group_count = lax.axis_size("win")
    run = LANES // (2 * window_count)
    slices = bin_count // (PARTS * LANES)
    table = jnp.asarray(lag_rows(bin_count, LAGS, window_count * group_count, slices))
    places = jnp.asarray(placement(spectra.shape[1]))
    return main(spectra, table, places, owners, blocks, max_lag, run)


def solution(mesh):
    return jax.shard_map(
        body,
        mesh=mesh,
        in_specs=(P("win", "chan", None, None), P(), P(), P(None, "win", "chan")),
        out_specs=P(None, "win", "chan", None),
        check_vma=False,
    )
```

```python
import functools

import jax
import jax.numpy as jnp
import numpy as np
from jax import lax
from jax.experimental import pallas as pl
from jax.experimental.pallas import tpu as pltpu
from jax.sharding import PartitionSpec as P

SRC = 16
STEPS = 4
LAGS = 128
LANES = 128
PARTS = 4
PAIRED = 2
KIB = 56 << 10


def lag_rows(bin_count, lag_count, window_count, slices):
    bins = np.arange(bin_count, dtype=np.int64)[None, :]
    offsets = np.arange(lag_count, dtype=np.int64)[:, None] - lag_count // 2
    phase = (bins * offsets % (2 * bin_count)) * (np.pi / bin_count)
    weight = np.where(bins == 0, 1.0, 2.0) / np.sqrt(2.0 * bin_count * window_count)
    rows = np.stack([weight * np.cos(phase), -weight * np.sin(phase)], 1)
    rows = rows.reshape(lag_count, 2, slices, bin_count // slices).transpose(2, 0, 1, 3)
    return rows.reshape(slices, lag_count, -1).astype(np.float32).astype(jnp.bfloat16)


def placement(receivers):
    places = np.zeros((2, 2, 2 * receivers, 4, receivers), np.float32)
    c = np.arange(receivers)
    for half in range(2):
        places[half, 0, 2 * c, half, c] = 1
        places[half, 0, 2 * c + 1, 2 + half, c] = -1
        places[half, 1, 2 * c + 1, half, c] = 1
        places[half, 1, 2 * c, 2 + half, c] = 1
    return places.reshape(4, 2 * receivers, 4 * receivers).astype(jnp.bfloat16)


def main_kernel(
    owners_ref, blocks_ref, spectra_in, lag_in, place_in, limit_ref, out_ref,
    spectra_ref, lag_ref, place_ref, loaded,
    own, weights, cross_spectra, made, arrived, got,
    sent, from_core, half, from_cross, quarter, from_low, from_high, to_high, to_low,
    core_send, core_recv, cross_send, cross_recv, up_send, up_recv,
    down_send, down_recv, share_send, share_recv, last_send, last_recv,
    sum_send, sum_recv,
    *, length, members, run,
):
    chunks, parts, paired, groups, sources, width = own.shape
    slices = lag_ref.shape[0]
    steps = chunks // slices * paired
    pairs = sources // 2
    windows, receivers, _, bins = spectra_ref.shape
    terms = 2 * windows
    kept = sources // members
    me = lax.axis_index("chan")
    win = lax.axis_index("win")
    line, cross, core = me // 4, (me // 2) % 2, me % 2
    core_peer = me + 1 - 2 * core
    cross_peer = me + 2 - 4 * cross
    mine = 2 * core + cross
    theirs = 2 * core + 1 - cross
    has_low, has_high = line > 0, line < length - 1
    near_low = line < length // 2

    def remote(src, dst, send, recv, peer):
        return pltpu.make_async_remote_copy(
            src_ref=src, dst_ref=dst, send_sem=send, recv_sem=recv,
            device_id={"chan": peer}, device_id_type=pl.DeviceIdType.MESH,
        )

    def to_core(s):
        part = own.at[s, pl.ds(2 * (1 - core), 2)]
        return remote(part, from_core.at[s], core_send.at[s], core_recv.at[s], core_peer)

    def to_cross(s):
        return remote(
            half.at[s, 1 - cross], from_cross.at[s], cross_send.at[s], cross_recv.at[s],
            cross_peer,
        )

    def go_up(s):
        return remote(to_high.at[s], from_low.at[s], up_send.at[s], up_recv.at[s], me + 4)

    def go_down(s):
        return remote(to_low.at[s], from_high.at[s], down_send.at[s], down_recv.at[s], me - 4)

    def share(s):
        ref = got.at[s, mine]
        return remote(ref, ref, share_send.at[s], share_recv.at[s], cross_peer)

    def last(s, which, index):
        ref = got.at[s, index]
        return remote(ref, ref, last_send.at[s, which], last_recv.at[s, which], core_peer)

    def add_up(s, j):
        peer = (win + j) % members
        return pltpu.make_async_remote_copy(
            src_ref=sent.at[s, pl.ds(peer * kept, kept)],
            dst_ref=arrived.at[s, j - 1],
            send_sem=sum_send.at[s, j - 1],
            recv_sem=sum_recv.at[s, j - 1],
            device_id={"win": peer},
            device_id_type=pl.DeviceIdType.MESH,
        )

    loads = [
        pltpu.make_async_copy(src, dst, loaded.at[k])
        for k, (src, dst) in enumerate(
            ((spectra_in, spectra_ref), (place_in, place_ref), (lag_in, lag_ref))
        )
    ]
    for load in loads:
        load.start()

    barrier = pltpu.get_barrier_semaphore()

    def greet(peer):
        pl.semaphore_signal(
            barrier, inc=1, device_id={"chan": peer}, device_id_type=pl.DeviceIdType.MESH
        )

    greet(core_peer)
    greet(cross_peer)
    for j in range(1, members):
        pl.semaphore_signal(
            barrier,
            inc=1,
            device_id={"win": (win + j) % members},
            device_id_type=pl.DeviceIdType.MESH,
        )

    @pl.when(has_low)
    def _():
        greet(me - 4)

    @pl.when(has_high)
    def _():
        greet(me + 4)

    pl.semaphore_wait(
        barrier, 1 + members + jnp.where(has_low, 1, 0) + jnp.where(has_high, 1, 0)
    )

    def single(s):
        return s >= chunks - paired

    def step_of(s, i):
        return jnp.where(single(s), s - chunks + steps, s // slices * paired + i)

    def slice_of(s, i):
        return jnp.where(single(s), slices - paired + i, s % slices)

    def choose(ref, s, mine_if, own, other):
        for i in range(paired):
            ref[s, i] = lax.select(mine_if(owners_ref[step_of(s, i)]), own[i], other[i])

    block = lax.broadcasted_iota(jnp.int32, (sources, LANES), 1) // run
    odd = [(block // bit) % 2 == 1 for bit in (1, 2, 4)]

    def choice(step):
        shape = (2 * sources, 2 * receivers)
        row = lax.broadcasted_iota(jnp.int32, shape, 0)
        column = lax.broadcasted_iota(jnp.int32, shape, 1)
        wanted = 2 * (blocks_ref[step] * sources + row % sources) + row // sources
        return jnp.where(column == wanted, 1.0, 0.0).astype(jnp.bfloat16)

    def channels(w, at, size):
        return spectra_ref[w, :, :, at].reshape(2 * receivers, size)

    def lay(s):
        for two in range(parts // 2):
            for j in range(paired):
                picks = choice(step_of(s, j))
                q = slice_of(s, j) * parts + 2 * two
                at = pl.ds(pl.multiple_of(q * LANES, 2 * LANES), 2 * LANES)
                found = [
                    jnp.dot(picks, channels(w, at, 2 * LANES), preferred_element_type=jnp.float32)
                    for w in range(windows)
                ]
                for e in range(2):
                    tiles = []
                    for i in range(terms):
                        top = i % 2 * sources
                        tile = found[i // 2][top : top + sources, e * LANES : (e + 1) * LANES]
                        tiles.append(pltpu.roll(tile, i * run, 1) if i else tile)
                    for k, mask in enumerate(odd):
                        tiles = [
                            jnp.where(mask, tiles[(i + (1 << k)) % terms], tiles[i])
                            for i in range(terms)
                        ]
                    wide = [
                        jnp.concatenate([tiles[-g % terms][:pairs], tiles[-g % terms][pairs:]], 1)
                        for g in range(2 * groups)
                    ]
                    for g in range(groups):
                        own[s, 2 * two + e, j, g] = jnp.concatenate(
                            wide[2 * g : 2 * g + 2], 0
                        ).astype(jnp.bfloat16)

    def leave(s):
        to_core(s).wait_recv()
        for i in range(paired):
            owner = owners_ref[step_of(s, i)]
            for k in range(2):
                half[s, k, i] = lax.select(
                    owner == me, own[s, 2 * core + k, i], from_core[s, k, i]
                )
        to_cross(s).start()

    loads[0].wait()

    @pl.loop(0, chunks + 1)
    def _(t):
        @pl.when(t < chunks)
        def _():
            lay(t)
            to_core(t).start()

        @pl.when(t >= 1)
        def _():
            leave(t - 1)

    def weigh(b):
        @pl.loop(0, PARTS)
        def _(part):
            q = b * PARTS + part
            at = pl.ds(pl.multiple_of(q * LANES, LANES), LANES)
            for w in range(windows):
                turned = channels(w, at, LANES).T
                for k in range(4):
                    tile = jnp.dot(
                        turned, place_ref[k], preferred_element_type=jnp.float32
                    ).astype(jnp.bfloat16)
                    for g in range(2 * groups):
                        row = (k // 2) * LANES + (2 * w + k % 2 + g) % terms * run
                        weights[q * 2 * groups + g, row : row + run] = tile[
                            g * run : (g + 1) * run
                        ]

    def limits():
        same = lax.broadcasted_iota(jnp.int32, (receivers, receivers), 0) == (
            lax.broadcasted_iota(jnp.int32, (receivers, receivers), 1)
        )
        for s in range(steps):
            for k in range(kept):
                line_of = limit_ref[s, k : k + 1].astype(jnp.float32)
                column = jnp.where(same, jnp.broadcast_to(line_of, same.shape), 0.0)
                column = jnp.sum(column, axis=1, keepdims=True)
                out_ref[s, k] = jnp.broadcast_to(column, out_ref.shape[2:])

    lane = lax.broadcasted_iota(jnp.int32, (run, width), 1) % run
    row = lax.broadcasted_iota(jnp.int32, (run, width), 0)
    keep = (lane == row).astype(jnp.float32)

    def spread(value, e):
        return [
            (jnp.broadcast_to(value[r : r + 1], (run, width)) * keep).astype(jnp.bfloat16)
            for r in range(e * pairs, (e + 1) * pairs)
        ]

    def multiply(rows, which):
        dots = jnp.dot(
            jnp.concatenate(rows, 0), weights[which], preferred_element_type=jnp.float32
        )
        return dots.astype(jnp.bfloat16)

    def keep_products(s, i, part, at, dots):
        base = pl.multiple_of((part * 2 * groups + at) * run, run)
        buffer, piece = step_of(s, i) % paired, slice_of(s, i)
        for p in range(pairs):
            one = dots[p * run : (p + 1) * run]
            to = slice(p * LANES, (p + 1) * LANES)
            cross_spectra[buffer, piece, 0, pl.ds(base, run), to] = one[:, :LANES]
            cross_spectra[buffer, piece, 1, pl.ds(base, run), to] = one[:, LANES:]

    def cross_part(s, part):
        first = (s % slices * parts + part) * 2 * groups
        for g in range(groups):
            values = [got[s, part, i, g].astype(jnp.float32) for i in range(paired)]
            for e in range(2):
                at = 2 * g + e
                dots = multiply(spread(values[0], e) + spread(values[1], e), first + at)
                for i in range(paired):
                    keep_products(s, i, part, at, dots[i * pairs * run : (i + 1) * pairs * run])

    def cross_single(s, part):
        for i in range(paired):
            first = (slice_of(s, i) * parts + part) * 2 * groups
            for g in range(groups):
                value = got[s, part, i, g].astype(jnp.float32)
                for e in range(2):
                    at = 2 * g + e
                    keep_products(s, i, part, at, multiply(spread(value, e), first + at))

    def lag_part(step, b, last_one):
        for n in range(pairs // 2):
            at = slice(n * 2 * LANES, (n + 1) * 2 * LANES)
            values = jnp.concatenate(
                [cross_spectra[step % paired, b + k // 2, k % 2, :, at] for k in range(4)], 0
            )
            table = jnp.concatenate([lag_ref[b], lag_ref[b + 1]], 1)
            turned = jnp.dot(table, values, preferred_element_type=jnp.float32).T
            for k in range(4):
                source = 2 * n + k // 2 + (k % 2) * pairs
                one = turned[k * receivers : (k + 1) * receivers]
                if not last_one:
                    made[step, source] = one
                    continue
                one += made[step, source]
                made[step, source] = one
                sent[step, source] = one.astype(jnp.bfloat16)
        if last_one:
            for j in range(1, members):
                add_up(step, j).start()

    def low_side(s):
        @pl.when(has_low)
        def _():
            go_up(s).wait_recv()
            choose(to_high, s, lambda o: o // 4 == line, quarter[s], from_low[s])

            @pl.when(has_high)
            def _():
                go_up(s).start()

    def high_side(s):
        @pl.when(has_high)
        def _():
            go_down(s).wait_recv()
            choose(to_low, s, lambda o: o // 4 == line, quarter[s], from_high[s])

            @pl.when(has_low)
            def _():
                go_down(s).start()

    def enter(s):
        to_cross(s).wait_recv()

        choose(quarter, s, lambda o: (o // 2) % 2 == cross, half[s, cross], from_cross[s])

        @pl.when(line == 0)
        def _():
            to_high[s] = quarter[s]
            go_up(s).start()

        @pl.when(line == length - 1)
        def _():
            to_low[s] = quarter[s]
            go_down(s).start()

    def near_side(s):
        @pl.when(near_low)
        def _():
            low_side(s)

        @pl.when(jnp.logical_not(near_low))
        def _():
            high_side(s)

    def far_side(s):
        @pl.when(near_low)
        def _():
            high_side(s)

        @pl.when(jnp.logical_not(near_low))
        def _():
            low_side(s)

    inner = (line > 0) & (line < length - 1)

    def settle(s):
        @pl.when(jnp.logical_not(inner))
        def _():
            far_side(s)

        choose(got.at[:, mine], s, lambda o: o // 4 <= line, to_high[s], to_low[s])
        share(s).start()
        last(s, 0, mine).start()

    def pass_on(s):
        share(s).wait_recv()
        last(s, 1, theirs).start()

    limits()
    loads[1].wait()
    loads[2].wait()

    def at(t, delay):
        return (t >= delay) & (t < chunks + delay)

    @pl.loop(0, chunks + 8)
    def _(t):
        @pl.when(t >= 8)
        def _():
            pass_on(t - 8)

        @pl.when(at(t, 6))
        def _():
            settle(t - 6)

        @pl.when(at(t, 4) & inner)
        def _():
            far_side(t - 4)

        @pl.when(at(t, 2))
        def _():
            near_side(t - 2)

        @pl.when(t < chunks)
        def _():
            enter(t)

        @pl.when(t < slices)
        def _():
            weigh(t)

        def finish(s, cross_of):
            cross_of(s, mine)
            cross_of(s, theirs)
            for which in range(2):
                last(s, which, mine).wait_recv()
            cross_of(s, 2 * (1 - core))
            cross_of(s, 2 * (1 - core) + 1)

        @pl.when((t >= 8) & (t - 8 < chunks - paired))
        def _():
            s = t - 8
            finish(s, cross_part)

            @pl.when(s % slices == slices // 2 - 1)
            def _():
                for i in range(paired):
                    lag_part(s // slices * paired + i, 0, False)

            @pl.when(s % slices == slices - 1)
            def _():
                for i in range(paired):
                    lag_part(s // slices * paired + i, slices - 2, True)

        @pl.when(t - 8 >= chunks - paired)
        def _():
            s = t - 8
            finish(s, cross_single)
            lag_part(step_of(s, 0), slices - 2, True)

    @pl.loop(0, steps - 1)
    def _(s):
        total = made[s, pl.ds(win * kept, kept)]
        for j in range(1, members):
            add_up(s, j).wait()
            total += arrived[s, j - 1].astype(jnp.float32)
        offset = lax.broadcasted_iota(jnp.int32, total.shape, 2) - total.shape[2] // 2
        inside = jnp.abs(offset).astype(jnp.float32) <= out_ref[s]
        out_ref[s] = jnp.where(inside, total, 0.0)

    @pl.loop(0, chunks)
    def _(s):
        to_core(s).wait_send()
        to_cross(s).wait_send()
        share(s).wait_send()
        for which in range(2):
            last(s, which, mine).wait_send()

        @pl.when(has_high)
        def _():
            go_up(s).wait_send()

        @pl.when(has_low)
        def _():
            go_down(s).wait_send()

    @pl.loop(steps - 1, steps)
    def _(s):
        total = made[s, pl.ds(win * kept, kept)]
        for j in range(1, members):
            add_up(s, j).wait()
            total += arrived[s, j - 1].astype(jnp.float32)
        offset = lax.broadcasted_iota(jnp.int32, total.shape, 2) - total.shape[2] // 2
        inside = jnp.abs(offset).astype(jnp.float32) <= out_ref[s]
        out_ref[s] = jnp.where(inside, total, 0.0)


def main(spectra, table, places, owners, blocks, max_lag, run):
    windows, receivers, _, bins = spectra.shape
    members = lax.axis_size("win")
    slices, lags, _ = table.shape
    steps, sources, dtype = STEPS, SRC, spectra.dtype
    chunks = steps // PAIRED * slices
    piece = (PAIRED, LANES // run // 2, sources, 2 * LANES)
    kept = (sources // members, receivers, lags)
    return pl.pallas_call(
        functools.partial(
            main_kernel, length=lax.axis_size("chan") // 4, members=members, run=run
        ),
        out_shape=jax.ShapeDtypeStruct((steps,) + kept, jnp.float32),
        in_specs=[pl.BlockSpec(memory_space=pltpu.SMEM)] * 2
        + [pl.BlockSpec(memory_space=pltpu.HBM)] * 3
        + [pl.BlockSpec(memory_space=pltpu.VMEM)],
        out_specs=pl.BlockSpec(memory_space=pltpu.VMEM),
        scratch_shapes=[
            pltpu.VMEM(spectra.shape, dtype),
            pltpu.VMEM(table.shape, dtype),
            pltpu.VMEM(places.shape, dtype),
            pltpu.SemaphoreType.DMA((3,)),
            pltpu.VMEM((chunks, PARTS) + piece, dtype),
            pltpu.VMEM((bins // run, 2 * LANES, 2 * LANES), dtype),
            pltpu.VMEM((PAIRED, slices, 2, bins // slices, sources // 2 * LANES), dtype),
            pltpu.VMEM((steps, sources, receivers, lags), jnp.float32),
            pltpu.VMEM((steps, members - 1) + kept, dtype),
            pltpu.VMEM((chunks, PARTS) + piece, dtype),
            pltpu.VMEM((steps, sources, receivers, lags), dtype),
            pltpu.VMEM((chunks, 2) + piece, dtype),
            pltpu.VMEM((chunks, 2) + piece, dtype),
        ]
        + [pltpu.VMEM((chunks,) + piece, dtype)] * 6
        + [pltpu.SemaphoreType.DMA((chunks,))] * 10
        + [pltpu.SemaphoreType.DMA((chunks, 2))] * 2
        + [pltpu.SemaphoreType.DMA((steps, members - 1))] * 2,
        compiler_params=pltpu.CompilerParams(
            collective_id=0, has_side_effects=True, vmem_limit_bytes=KIB << 10
        ),
    )(owners, blocks, spectra, table, places, max_lag)


def body(spectra, owners, blocks, max_lag):
    window_count, _, _, bin_count = spectra.shape
    group_count = lax.axis_size("win")
    run = LANES // (2 * window_count)
    slices = bin_count // (PARTS * LANES)
    table = jnp.asarray(lag_rows(bin_count, LAGS, window_count * group_count, slices))
    places = jnp.asarray(placement(spectra.shape[1]))
    return main(spectra, table, places, owners, blocks, max_lag, run)


def solution(mesh):
    return jax.shard_map(
        body,
        mesh=mesh,
        in_specs=(P("win", "chan", None, None), P(), P(), P(None, "win", "chan")),
        out_specs=P(None, "win", "chan", None),
        check_vma=False,
    )
```
